128 devices in a mesh: gx: 16 (over z_lo, y, core), gy: 8 (over x, z_hi).
Axes of the slice: x: 4, y: 4, z: 4 (z_hi: 2, z_lo: 2; z = z_hi * 2 + z_lo), core: 2. Of those that a mesh axis runs over, the one named last changes fastest.
Arguments:
- field_e: float32 [3, 256, 128, 256], P(None, 'gx', 'gy'), may hold values from -6 to 6
- field_h: float32 [3, 256, 128, 256], P(None, 'gx', 'gy'), may hold values from -6 to 6
- density: float32 [2, 8, 8, 2097152], P(None, None, None, ('gx', 'gy')), may hold values from -1.8 to 1.8
- dipole: float32 [3, 2097152], P(None, ('gx', 'gy')), may hold values from -6 to 6
- levels: float32 [8], replicated, may hold values from -3 to 3
- coupling: float32 [8, 8], replicated, may hold values from -2 to 2
- rates: float32 [8, 8], replicated, may hold values from 0.1 to 3
- tile_cells: int32 [16384], P(('gx', 'gy')), may hold values from 0 to 511, as said below
- tile_owner: int32 [16384, 1], P(('gx', 'gy')), may hold values from 0 to 127; in each aligned block of 128 rows (0 to 127, 128 to 255, ...) at most 2 rows name the same one
- emitter_offsets: int32 [16384, 64], P(('gx', 'gy')), may hold values from 0 to 127
Outputs:
- electric_out: float32 [3, 256, 128, 256], P(None, 'gx', 'gy')
- magnetic_out: float32 [3, 256, 128, 256], P(None, 'gx', 'gy')
- density_out: float32 [2, 8, 8, 2097152], P(None, None, None, ('gx', 'gy'))
The draws below stay inside these ranges and needn't reach their ends.
Inputs may be any that keep to these rules, and one draw needn't show every extreme that they name: `tile_cells`: within one device's 128 entries the local tile numbers are distinct. `tile_owner`: among the 128 tiles of one device no owner is named more than 2 times.
All inputs are finite; a program needn't handle non-finite values.
Results may differ from the reference program's by a relative error of at most 0.0003.
Values sent between devices are 32-bit elements; how exact they have to be, the bound alone decides.
A program may use at most 320 MiB of HBM per device.

```python
import math
import jax
import jax.numpy as jnp
import numpy as np
from jax import lax

CX = 16
CY = 16
NZ = 256
TILE = 128
LEVELS = 8
EMIT = 64
TILE_DEV = 128
STEPS = 4
NX = 256
NY = 128
NZB = 2
CAP = 2
SLOTS_DEV = 16384
EMITTERS_ALL = 2097152
TILES_ALL = 16384
N_GX = 16
N_GY = 8


def draw_tile_cells(key, part):
    devices = TILES_ALL // TILE_DEV
    columns = CX * CY * NZB

    def one_device(subkey):
        key_pick, key_order = jax.random.split(subkey)
        middle = jax.random.permutation(key_pick, columns - 2)[:TILE_DEV - 2].astype(jnp.int32) + 1
        chosen = jnp.concatenate([jnp.array([0, columns - 1], jnp.int32), middle])
        return jax.random.permutation(key_order, chosen)
    return jax.vmap(one_device)(jax.random.split(key, devices)).reshape(-1).astype(jnp.int32)


def set_ends(entries, own_key, low, top_value):
    index_at = [jax.random.randint(jax.random.fold_in(own_key, axis), (), 0, length) for axis, length in enumerate(entries.shape)]
    widest = entries.shape.index(max(entries.shape))
    beside = index_at[:widest] + [(index_at[widest] + 1) % entries.shape[widest]] + index_at[widest + 1:]
    return entries.at[tuple(index_at)].set(low).at[tuple(beside)].set(top_value)


def block_scale(key, extent, cuts, smallest, high):
    def one(position, parts):
        draws = jax.random.uniform(jax.random.fold_in(jax.random.fold_in(key, 6), position), (parts,), jnp.float32, smallest / len(cuts), high / len(cuts))
        return jnp.repeat(jnp.exp(draws), extent[position] // parts).reshape((-1,) + (1,) * (len(extent) - position - 1))

    loudness = one(*cuts[0])
    for cut in cuts[1:]:
        loudness = loudness * one(*cut)
    return loudness


def routed_block(stream_key, own, number, rows, count, top, bound, lean):
    order = jax.random.permutation(stream_key, count)
    packed, usual = load_shares(count, rows * top, bound, lean, True), load_shares(count, rows * top, bound, lean, False)
    places = jnp.arange(count)

    def named(tallies, rotation):
        used = int((tallies > 0).sum())
        fixed = max(1, used // 4)
        moved = fixed + (places - fixed + rotation * (used - fixed)) % max(1, count - fixed)
        return jnp.zeros((count,), jnp.int32).at[order[jnp.where(places < fixed, places, moved)]].set(jnp.asarray(tallies, jnp.int32))

    tallies = jnp.where(number % 4 == 0, named(packed, number // 4), named(usual, number - number // 4 - 1))
    mixed = jax.random.permutation(jax.random.fold_in(own, 3), count)
    source_of, taker = mixed[0:count // 2 * 2:2], mixed[1:count // 2 * 2:2]
    margin = jnp.minimum(tallies[source_of] - 1, bound - tallies[taker]) // 2
    margin = jnp.where((source_of == order[0]) | (taker == order[0]) | (tallies[taker] == 0), 0, jnp.maximum(margin, 0))
    moved = jax.random.randint(jax.random.fold_in(own, 4), (count // 2,), 0, 1 << 20) % (margin + 1)
    tallies = tallies.at[source_of].add(-moved).at[taker].add(moved)
    items = jnp.searchsorted(jnp.cumsum(tallies), jnp.arange(rows * top), side="right").astype(jnp.int32)
    listing = items.reshape(top, rows).T
    listing = listing[jax.random.permutation(jax.random.fold_in(own, 1), rows)]
    rotation = jax.random.randint(jax.random.fold_in(own, 2), (rows, 1), 0, top)
    return jnp.take_along_axis(listing, (jnp.arange(top)[None, :] + rotation) % top, axis=1)


def load_shares(count, total, reach, lean, full):
    loads = [(1 << 20) // math.isqrt(rank ** lean) + 1 for rank in range(1, count + 1)]
    largest = reach if full else min(reach, max(-(-total // count), total * loads[0] // sum(loads)))
    least = 1 if total - largest >= count - 1 else 0
    holding, rest = [largest] + [least] * (count - 1), total - largest - least * (count - 1)
    while rest > 0:
        movable = [i for i in range(1, count) if holding[i] < largest] or [i for i in range(1, count) if holding[i] < reach]
        whole, left = sum([loads[i] for i in movable]), rest
        for i in movable:
            more = min(reach - holding[i], max(1, left * loads[i] // whole), rest)
            holding[i] = holding[i] + more
            rest = rest - more
    return np.array(holding)


def bell_draw(stream_key, extent, scale, reach, pieces=(), kind=jnp.bfloat16):
    values = jax.random.normal(stream_key, extent, jnp.float32) * scale
    if len(pieces) > 0:
        values = block_scale(stream_key, extent, pieces, -0.22, 0.18) * values
    return jnp.clip(values, min=-reach, max=reach).astype(kind)


def setup_inputs(seed: int = 0) -> dict:
    keys = jax.random.split(jax.random.key(seed), 11)
    field_e = bell_draw(keys[0], (3, NX, NY, NZ), 1.0, 6.0, ((1, 16), (2, 8)), jnp.float32)
    field_h = bell_draw(keys[1], (3, NX, NY, NZ), 1.0, 6.0, ((1, 16), (2, 8)), jnp.float32)
    density = bell_draw(keys[2], (2, LEVELS, LEVELS, EMITTERS_ALL), 0.3, 1.8, ((3, 128),), jnp.float32)
    dipole = bell_draw(keys[3], (3, EMITTERS_ALL), 1.0, 6.0, ((1, 128),), jnp.float32)
    levels = jnp.clip(jax.random.uniform(keys[4], (LEVELS,), jnp.float32, -3.0, 3.0), -3.0, 3.0)
    coupling = bell_draw(keys[5], (LEVELS, LEVELS), LEVELS ** -0.5, 2.0, (), jnp.float32)
    rates = jnp.clip(jnp.exp(jax.random.uniform(keys[6], (LEVELS, LEVELS), jnp.float32, math.log(0.1), math.log(3.0))), 0.1, 3.0)
    tile_cells = draw_tile_cells(jax.random.fold_in(keys[10], 71), 0)
    tile_owner_keys = jax.random.split(jax.random.fold_in(keys[8], 1), TILES_ALL // TILE_DEV)
    tile_owner_turns = jax.random.permutation(jax.random.fold_in(keys[8], 3), TILES_ALL // TILE_DEV)
    tile_owner = jax.vmap(lambda own, number: routed_block(jax.random.fold_in(keys[8], 2), own, number, TILE_DEV, N_GX * N_GY, 1, CAP, 2))(tile_owner_keys, tile_owner_turns).reshape((TILES_ALL, 1))
    emitter_offsets = set_ends(jax.random.randint(keys[9], (TILES_ALL, EMIT), 0, TILE), jax.random.fold_in(keys[9], 1), 0, TILE - 1).astype(jnp.int32)
    return dict(field_e=field_e, field_h=field_h, density=density, dipole=dipole, levels=levels, coupling=coupling, rates=rates, tile_cells=tile_cells, tile_owner=tile_owner, emitter_offsets=emitter_offsets)


courant = 0.5
time_step = 0.12


def forward(values_in, beyond, along):
    length = values_in.shape[along]
    return jnp.concatenate([lax.slice_in_dim(values_in, 1, length, axis=along), beyond], axis=along) - values_in


def backward(values_in, behind_slab, along):
    length = values_in.shape[along]
    return values_in - jnp.concatenate([behind_slab, lax.slice_in_dim(values_in, 0, length - 1, axis=along)], axis=along)


def zero_edge(values_in, along):
    return jnp.zeros_like(lax.slice_in_dim(values_in, 0, 1, axis=along))


def curl_ahead(fields, planes, rows):
    curl_one = forward(fields[2], rows[1], 1) - forward(fields[1], zero_edge(fields[1], 2), 2)
    curl_two = forward(fields[0], zero_edge(fields[0], 2), 2) - forward(fields[2], planes[1], 0)
    curl_three = forward(fields[1], planes[0], 0) - forward(fields[0], rows[0], 1)
    return jnp.stack([curl_one, curl_two, curl_three])


def curl_behind(fields, planes, rows):
    curl_one = backward(fields[2], rows[1], 1) - backward(fields[1], zero_edge(fields[1], 2), 2)
    curl_two = backward(fields[0], zero_edge(fields[0], 2), 2) - backward(fields[2], planes[1], 0)
    curl_three = backward(fields[1], planes[0], 0) - backward(fields[0], rows[0], 1)
    return jnp.stack([curl_one, curl_two, curl_three])


def commutator(symmetric, matrix):
    result = jnp.zeros_like(matrix)
    for inner in range(matrix.shape[0]):
        result = result + symmetric[:, inner][:, None, None] * matrix[inner][None, :, :]
        result = result - matrix[:, inner][:, None, :] * symmetric[inner][None, :, None]
    return result


def advance(states, orient, samples, levels, symmetric, damping):
    real_part = states[0]
    imag_part = states[1]
    driving = orient[0] * samples[0] + orient[1] * samples[1] + orient[2] * samples[2]
    spacing = (levels[:, None] - levels[None, :])[:, :, None]
    decays = damping[:, :, None]
    comm_imag = commutator(symmetric, imag_part)
    comm_real = commutator(symmetric, real_part)
    change_real = spacing * imag_part + driving * comm_imag - decays * real_part
    change_imag = -spacing * real_part - driving * comm_real - decays * imag_part
    moved = time_step * jnp.sum(symmetric[:, :, None] * change_real, axis=(0, 1))
    updated = jnp.stack([real_part + time_step * change_real, imag_part + time_step * change_imag])
    return updated, moved[None, :] * orient


def reference(field_e, field_h, density, dipole, levels, coupling, rates, tile_cells, tile_owner, emitter_offsets):
    devices = N_GX * N_GY
    symmetric = 0.5 * (coupling + coupling.T)
    damping = 0.5 * (rates + rates.T) * (1.0 - jnp.eye(LEVELS, dtype=jnp.float32))
    owners = tile_owner[:, 0].reshape(devices, TILE_DEV)
    ordinal = jnp.arange(TILE_DEV, dtype=jnp.int32)
    earlier = ordinal[None, :] < ordinal[:, None]
    matches = owners[:, :, None] == owners[:, None, :]
    ranking = jnp.sum(jnp.where(matches & earlier[None], 1, 0), axis=2).astype(jnp.int32)
    source = jnp.arange(devices, dtype=jnp.int32)[:, None]
    within = jnp.arange(EMIT, dtype=jnp.int32)
    slot_index = ((owners * SLOTS_DEV + (source * CAP + ranking) * EMIT)[:, :, None] + within).reshape(-1).astype(jnp.int32)
    tile_ids = tile_cells.reshape(devices, TILE_DEV)
    column = tile_ids // NZB
    grid_x = (source // N_GY) * CX + column // CY
    grid_y = (source % N_GY) * CY + column % CY
    grid_z = ((tile_ids % NZB) * TILE)[:, :, None] + emitter_offsets.reshape(devices, TILE_DEV, EMIT)
    cell_index = (((grid_x * NY + grid_y) * NZ)[:, :, None] + grid_z).reshape(-1).astype(jnp.int32)
    zero_planes = jnp.zeros((2, 1, NY, NZ), jnp.float32)
    zero_rows = jnp.zeros((2, NX, 1, NZ), jnp.float32)
    for repeat in range(STEPS):
        field_h = field_h - courant * curl_ahead(field_e, zero_planes, zero_rows)
        field_e = field_e + courant * curl_behind(field_h, zero_planes, zero_rows)
        flattened = field_e.reshape(3, -1)
        gathered = jnp.zeros((3, EMITTERS_ALL), jnp.float32).at[:, slot_index].set(flattened[:, cell_index])

        def owner_block(owner_index, carry):
            states, feed_terms = carry
            offset_start = (owner_index * SLOTS_DEV).astype(jnp.int32)
            segment = lax.dynamic_slice_in_dim(states, offset_start, SLOTS_DEV, axis=3)
            orient = lax.dynamic_slice_in_dim(dipole, offset_start, SLOTS_DEV, axis=1)
            samples = lax.dynamic_slice_in_dim(gathered, offset_start, SLOTS_DEV, axis=1)
            updated, feed_block = advance(segment, orient, samples, levels, symmetric, damping)
            states = lax.dynamic_update_slice_in_dim(states, updated, offset_start, axis=3)
            feed_terms = lax.dynamic_update_slice_in_dim(feed_terms, feed_block, offset_start, axis=1)
            return states, feed_terms

        density, feed_terms = lax.fori_loop(0, devices, owner_block, (density, jnp.zeros((3, EMITTERS_ALL), jnp.float32)))
        flattened = flattened.at[:, cell_index].add(-feed_terms[:, slot_index])
        field_e = flattened.reshape(field_e.shape)
    return field_e, field_h, density
```

```python
import functools

import jax
import jax.numpy as jnp
from jax import lax
from jax.experimental import pallas as pl
from jax.experimental.pallas import tpu as pltpu
from jax.sharding import PartitionSpec as P

TILE = 128
STEPS = 4
COURANT = 0.5
TIME_STEP = 0.12

MESH = pl.DeviceIdType.MESH
F32 = jnp.float32
BF16 = jnp.bfloat16


def iota(shape, axis):
    return lax.broadcasted_iota(jnp.int32, shape, axis)


def lanes_at(values, index):
    return jnp.take_along_axis(values, index, axis=1, mode="promise_in_bounds")


def split(values):
    high = values.astype(BF16)
    return high, (values - high.astype(F32)).astype(BF16)


def product(left, right):
    return jnp.dot(left, right, preferred_element_type=F32)


def exact(left, right):
    return jnp.dot(left, right, preferred_element_type=F32, precision=lax.Precision.HIGHEST)


def exact_t(left, right):
    return lax.dot_general(
        left,
        right,
        (((1,), (1,)), ((), ())),
        preferred_element_type=F32,
        precision=lax.Precision.HIGHEST,
    )


def shift_rows(values, amount):
    return pltpu.roll(values, amount % values.shape[0], 0)


def shift_lanes(values, amount):
    return pltpu.roll(values, amount % values.shape[1], 1)


def level_constants(levels, coupling, rates, size):
    pairs = size * size
    first = jnp.where(iota((pairs, size), 0) // size == iota((pairs, size), 1), 1.0, 0.0).astype(F32)
    second = jnp.where(iota((pairs, size), 0) % size == iota((pairs, size), 1), 1.0, 0.0).astype(F32)
    row_at, col_at = iota((pairs, pairs), 0), iota((pairs, pairs), 1)
    eye = jnp.where(row_at == col_at, 1.0, 0.0).astype(F32)

    def pair_of(pick):
        half = exact(pick, coupling)
        return 0.5 * (exact_t(half, pick) + exact_t(pick, half))

    def symmetrized(values):
        return 0.5 * (
            jnp.sum(exact(first, values) * second, axis=1, keepdims=True)
            + jnp.sum(exact(second, values) * first, axis=1, keepdims=True)
        )

    def as_row(column):
        return jnp.sum(eye * column, axis=0, keepdims=True)

    commute = jnp.where(row_at % size == col_at % size, pair_of(first), 0.0) - jnp.where(
        row_at // size == col_at // size, pair_of(second), 0.0
    )
    sym = symmetrized(coupling)
    off_diagonal = jnp.where(
        iota((pairs, 1), 0) // size == iota((pairs, 1), 0) % size, 0.0, 1.0
    ).astype(F32)
    decay = TIME_STEP * symmetrized(rates) * off_diagonal
    spacing = TIME_STEP * jnp.sum((first - second) * levels, axis=1, keepdims=True)

    sym_row, decay_row, spacing_row = as_row(sym), as_row(decay), as_row(spacing)
    rows = iota((8, pairs), 0)

    def free(real, imag):
        keep = 1.0 - decay_row
        return real * keep - imag * spacing_row, real * spacing_row + imag * keep

    def driven(real, imag):
        return -exact(imag, commute), exact(real, commute)

    def both(real, imag, distance):
        free_real, free_imag = free(real, imag)
        driven_real, driven_imag = driven(real, imag)
        return (
            free_real + shift_rows(driven_real, distance),
            free_imag + shift_rows(driven_imag, distance),
        )

    push = exact(jnp.broadcast_to(sym_row, (8, pairs)), commute)
    real_zero = jnp.where(rows == 0, -sym_row * decay_row, 0.0)
    imag_zero = jnp.where(rows == 0, sym_row * spacing_row, jnp.where(rows == 1, push, 0.0))
    real_one, imag_one = both(real_zero, imag_zero, 2)
    real_two, imag_two = both(real_one, imag_one, 4)

    def parts(matrix):
        high, low = split(matrix)
        return jnp.concatenate([high, high, low], axis=1)

    begin = parts(
        jnp.concatenate(
            [real_one + shift_rows(real_zero, 4), imag_one + shift_rows(imag_zero, 4)], axis=0
        )
    )
    later = parts(jnp.concatenate([commute, real_two, imag_two], axis=0))
    keep = jnp.broadcast_to(1.0 - decay, (pairs, TILE))
    spacing = jnp.broadcast_to(spacing, (pairs, TILE))
    return begin, later, keep, spacing


def kernel(
    gx,
    gy,
    cx,
    cy,
    levels_in,
    coupling_in,
    rates_in,
    cells_in,
    owner_in,
    offsets_in,
    e_in,
    h_in,
    dens_in,
    dip_in,
    e_out,
    h_out,
    dens_out,
    dens,
    dip_mine,
    pick,
    unpick,
    off_ref,
    perm_ref,
    last_ref,
    some_ref,
    same_ref,
    begin_ref,
    later_ref,
    keep_ref,
    spacing_ref,
    ep,
    hp,
    row_e,
    row_h,
    halo_e,
    halo_h,
    dip_send,
    dip_recv,
    drive_send,
    drive_recv,
    coef_send,
    coef_recv,
    coef_next,
    halo_send,
    halo_recv,
    dip_sems,
    drive_ssem,
    drive_rsem,
    coef_ssem,
    coef_rsem,
    in_sem,
    out_sem,
    field_sem,
):
    mx = lax.axis_index("gx")
    my = lax.axis_index("gy")
    me = mx * gy + my
    count = gx * gy
    plane = cy
    cols = cx * cy
    nz = 2 * TILE
    group = gy * TILE
    size = levels_in.shape[1]
    pairs = size * size

    def load_group(g):
        part = pl.ds(pl.multiple_of(g * group, group), group)
        return pltpu.make_async_copy(dens_in.at[:, part], dens.at[:, part], in_sem.at[g])

    def store_group(g):
        part = pl.ds(pl.multiple_of(g * group, group), group)
        return pltpu.make_async_copy(dens.at[:, part], dens_out.at[:, part], out_sem.at[g])

    field_loads = (
        pltpu.make_async_copy(e_in, ep.at[:, 0:cols, :], field_sem.at[0]),
        pltpu.make_async_copy(h_in, hp.at[:, plane : plane + cols, :], field_sem.at[1]),
    )
    field_stores = (
        pltpu.make_async_copy(ep.at[:, 0:cols, :], e_out, field_sem.at[0]),
        pltpu.make_async_copy(hp.at[:, plane : plane + cols, :], h_out, field_sem.at[1]),
    )
    dip_load = pltpu.make_async_copy(dip_in, dip_mine, field_sem.at[2])

    def along_x(j):
        return lax.rem(mx + j, gx)

    def along_y(j):
        return lax.rem(my + j, gy)

    def device_of(number):
        return number // gy, lax.rem(number, gy)

    def to_all(source, target, base, step_of, width, send_sem, recv_sem):
        def one(j, carry):
            peer = lax.rem(me + j, count)
            pltpu.make_async_remote_copy(
                src_ref=source.at[pl.ds(base + peer * step_of, width), :],
                dst_ref=target.at[pl.ds(base + me * step_of, width), :],
                send_sem=send_sem,
                recv_sem=recv_sem,
                device_id=device_of(peer),
                device_id_type=MESH,
            ).start()
            return carry

        lax.fori_loop(1, count, one, 0, unroll=8)
        own = pl.ds(base + me * step_of, width)
        target[own, :] = source[own, :]

    def whole(source, target, base, width, send_sem, recv_sem):
        rows = pl.ds(base, (count - 1) * width)
        return pltpu.make_async_remote_copy(
            src_ref=source.at[rows, :],
            dst_ref=target.at[rows, :],
            send_sem=send_sem,
            recv_sem=recv_sem,
            device_id=(along_x(1), my),
            device_id_type=MESH,
        )

    def all_drive(step):
        return whole(
            drive_send, drive_recv, step * count, 1, drive_ssem.at[step], drive_rsem.at[step]
        )

    def all_coef(step):
        return whole(
            coef_send, coef_recv, step * 2 * count, 2, coef_ssem.at[step], coef_rsem.at[step]
        )

    all_dip = whole(dip_send, dip_recv, 0, 4, dip_sems.at[0], dip_sems.at[1])

    x_below, x_above = along_x(gx - 1), along_x(1)
    y_below, y_above = along_y(gy - 1), along_y(1)

    def halo_copy(which, source, target, device):
        return pltpu.make_async_remote_copy(
            src_ref=source,
            dst_ref=target,
            send_sem=halo_send.at[which],
            recv_sem=halo_recv.at[which],
            device_id=device,
            device_id_type=MESH,
        )

    e_plane = halo_copy(
        0, ep.at[1:3, 0:plane, :], ep.at[1:3, cols : cols + plane, :], (x_below, my)
    )
    e_row = halo_copy(1, row_e, halo_e, (mx, y_below))
    h_plane = halo_copy(
        2, hp.at[1:3, cols : cols + plane, :], hp.at[1:3, 0:plane, :], (x_above, my)
    )
    h_row = halo_copy(3, row_h, halo_h, (mx, y_above))

    def send_e():
        for x in range(cx):
            row_e[0, x : x + 1, :] = ep[0, x * plane : x * plane + 1, :]
            row_e[1, x : x + 1, :] = ep[2, x * plane : x * plane + 1, :]
        e_row.start()
        e_plane.start()

    for copy in field_loads:
        copy.start()
    dip_load.start()

    @pl.loop(0, gx)
    def _(g):
        load_group(g).start()

    barrier = pltpu.get_barrier_semaphore()

    def greet(j, carry):
        pl.semaphore_signal(
            barrier, inc=1, device_id=device_of(lax.rem(me + j, count)), device_id_type=MESH
        )
        return carry

    lax.fori_loop(1, count, greet, 0, unroll=8)

    dip_load.wait()

    def dip_row(s, carry):
        lanes = pl.ds(pl.multiple_of(s * TILE, TILE), TILE)
        dip_send[pl.ds(pl.multiple_of(s * 4, 4), 3), :] = dip_mine[:, lanes]
        return carry

    dip_send[pl.ds(3, count, stride=4), :] = jnp.zeros((count, TILE), F32)
    lax.fori_loop(0, count, dip_row, 0, unroll=8)
    for copy in field_loads:
        copy.wait()

    pl.semaphore_wait(barrier, count - 1)
    send_e()
    to_all(dip_send, dip_recv, 0, 4, 4, dip_sems.at[0], dip_sems.at[1])

    begin, later, keep, spacing = level_constants(
        levels_in[...], coupling_in[...], rates_in[...], size
    )
    begin_ref[...] = begin
    later_ref[...] = later
    keep_ref[...] = keep
    spacing_ref[...] = spacing

    def stacked(real, imag):
        real_high, real_low = split(real)
        imag_high, imag_low = split(imag)
        high = jnp.concatenate([real_high, imag_high], axis=1)
        low = jnp.concatenate([real_low, imag_low], axis=1)
        return jnp.concatenate([high, low, high], axis=0)

    @pl.loop(0, gx)
    def _(g):
        load_group(g).wait()

    def first_look(s, carry):
        part = pl.ds(pl.multiple_of(s * TILE, TILE), TILE)
        seen = product(begin_ref[...], stacked(dens[0:pairs, part], dens[pairs : 2 * pairs, part]))
        coef_next[pl.ds(pl.multiple_of(s * 8, 8), 8), :] = seen[0:8, 0:TILE] + seen[8:16, TILE:]
        return carry

    lax.fori_loop(0, count, first_look, 0, unroll=4)

    def send_coef(step, alpha, beta):
        base = step * 2 * count
        coef_send[pl.ds(base, count, stride=2), :] = alpha
        coef_send[pl.ds(base + 1, count, stride=2), :] = beta
        to_all(coef_send, coef_recv, base, 2, 2, coef_ssem.at[step], coef_rsem.at[step])

    send_coef(
        0, coef_next[pl.ds(4, count, stride=8), :], coef_next[pl.ds(5, count, stride=8), :]
    )

    lane = iota((count, TILE), 1)
    sub = iota((count, TILE), 0)

    def find_places():
        eye = jnp.where(lane == sub, 1.0, 0.0).astype(F32)

        def column_of(row):
            return jnp.sum(eye * row, axis=1, keepdims=True)

        owner_row = owner_in[...].astype(F32)
        owner_col = column_of(owner_row)
        tiles = cells_in[...]
        cell_row = ((tiles & 1) * cols + (tiles >> 1)).astype(F32)
        cell_col = column_of(cell_row)
        alike = jnp.where(owner_col == owner_row, 1.0, 0.0)
        rank_col = jnp.sum(jnp.where(lane < sub, alike, 0.0), axis=1, keepdims=True)
        rank_row = jnp.sum(jnp.where(sub < lane, alike, 0.0), axis=0, keepdims=True)

        def flags(condition):
            return jnp.where(condition, 1.0, 0.0).astype(BF16)

        named = owner_row == sub.astype(F32)
        slot_zero = flags(named & (rank_row == 0.0))
        slot_one = flags(named & (rank_row == 1.0))
        taking = owner_col == lane.astype(F32)
        slot_zero_t = flags(taking & (rank_col == 0.0))
        slot_one_t = flags(taking & (rank_col == 1.0))
        at_cell = flags(cell_col == iota((count, 2 * cols), 1).astype(F32))
        at_cell_t = flags(cell_row == iota((2 * cols, count), 0).astype(F32))
        pick[0:count, :] = product(slot_zero, at_cell).astype(BF16)
        pick[count : 2 * count, :] = product(slot_one, at_cell).astype(BF16)
        unpick[:, 0:count] = product(at_cell_t, slot_zero_t).astype(BF16)
        unpick[:, count : 2 * count] = product(at_cell_t, slot_one_t).astype(BF16)

        offsets = offsets_in[...].astype(F32)
        offsets = jnp.concatenate([offsets, offsets], axis=1).astype(BF16)
        off = jnp.where(lane < TILE // 2, product(slot_zero, offsets), product(slot_one, offsets))
        off = off.astype(jnp.int32)
        off_ref[...] = off

        half = TILE // 2
        place = lane & (half - 1)
        base = lane & half
        key = off * half + place
        length = 2
        while length <= half:
            d = length // 2
            while d >= 1:
                partner = lanes_at(key, lane ^ d)
                lower = jnp.where((lane & d) == 0, 1, 0)
                upward = jnp.where((place & length) == 0, 1, 0)
                key = jnp.where(
                    lower == upward, jnp.minimum(key, partner), jnp.maximum(key, partner)
                )
                d //= 2
            length *= 2
        perm_ref[...] = base | (key & (half - 1))
        ordered = key >> 6
        d = 1
        level = 0
        while d < half:
            together = (place >= d) & (shift_lanes(ordered, d) == ordered)
            same_ref[level] = jnp.where(together, 1.0, 0.0).astype(F32)
            d *= 2
            level += 1
        for k in range(2):
            found = jnp.zeros((count, TILE), jnp.int32)
            jump = half // 2
            while jump >= 1:
                seen = lanes_at(ordered, found + (k * half + jump - 1))
                found = jnp.where(seen <= lane, found + jump, found)
                jump //= 2
            seen = lanes_at(ordered, found + k * half)
            found = jnp.where(seen <= lane, found + 1, found)
            last = jnp.maximum(found - 1, 0) + k * half
            hit = (found > 0) & (lanes_at(ordered, last) == lane)
            last_ref[k] = last
            some_ref[k] = jnp.where(hit, 1.0, 0.0).astype(F32)

    row_at = iota((plane, nz), 0)
    z_at = iota((plane, nz), 1)

    def next_y(values, row):
        return jnp.where(row_at == plane - 1, row, shift_rows(values, -1))

    def prior_y(values, row):
        return jnp.where(row_at == 0, row, shift_rows(values, 1))

    def next_z(values):
        return jnp.where(z_at == nz - 1, 0.0, shift_lanes(values, -1))

    def prior_z(values):
        return jnp.where(z_at == 0, 0.0, shift_lanes(values, 1))

    def step_h():
        keep_x = jnp.where(mx == gx - 1, 0.0, 1.0).astype(F32)
        keep_y = jnp.where(my == gy - 1, 0.0, 1.0).astype(F32)
        for c in (1, 2):
            ep[c, cols : cols + plane, :] = ep[c, cols : cols + plane, :] * keep_x
        for x in range(cx):
            here = slice(x * plane, (x + 1) * plane)
            after = slice((x + 1) * plane, (x + 2) * plane)
            e0, e1, e2 = ep[0, here, :], ep[1, here, :], ep[2, here, :]
            e1_x, e2_x = ep[1, after, :], ep[2, after, :]
            e0_y = next_y(e0, halo_e[0, x : x + 1, :] * keep_y)
            e2_y = next_y(e2, halo_e[1, x : x + 1, :] * keep_y)
            hp[0, after, :] = hp[0, after, :] - COURANT * ((e2_y - e2) - (next_z(e1) - e1))
            hp[1, after, :] = hp[1, after, :] - COURANT * ((next_z(e0) - e0) - (e2_x - e2))
            hp[2, after, :] = hp[2, after, :] - COURANT * ((e1_x - e1) - (e0_y - e0))
            bottom = slice((x + 2) * plane - 1, (x + 2) * plane)
            row_h[0, x : x + 1, :] = hp[0, bottom, :]
            row_h[1, x : x + 1, :] = hp[2, bottom, :]

    def step_e():
        hold_x = jnp.where(mx == 0, 0.0, 1.0).astype(F32)
        hold_y = jnp.where(my == 0, 0.0, 1.0).astype(F32)
        for c in (1, 2):
            hp[c, 0:plane, :] = hp[c, 0:plane, :] * hold_x
        for x in range(cx):
            here = slice(x * plane, (x + 1) * plane)
            after = slice((x + 1) * plane, (x + 2) * plane)
            h0, h1, h2 = hp[0, after, :], hp[1, after, :], hp[2, after, :]
            h1_x, h2_x = hp[1, here, :], hp[2, here, :]
            h0_y = prior_y(h0, halo_h[0, x : x + 1, :] * hold_y)
            h2_y = prior_y(h2, halo_h[1, x : x + 1, :] * hold_y)
            ep[0, here, :] = ep[0, here, :] + COURANT * ((h2 - h2_y) - (h1 - prior_z(h1)))
            ep[1, here, :] = ep[1, here, :] + COURANT * ((h0 - prior_z(h0)) - (h2 - h2_x))
            ep[2, here, :] = ep[2, here, :] + COURANT * ((h1 - h1_x) - (h0 - h0_y))

    def dipole_rows(c):
        return dip_recv[pl.ds(c, count, stride=4), :]

    def sampled_drive():
        drive = jnp.zeros((count, TILE), F32)
        for c in range(3):
            rows = jnp.zeros((2 * count, 2 * TILE), F32)
            for h in range(2):
                parts = jnp.concatenate(split(ep[c, 0:cols, h * TILE : (h + 1) * TILE]), axis=1)
                rows = rows + product(pick[:, h * cols : (h + 1) * cols], parts)
            rows = rows[:, 0:TILE] + rows[:, TILE : 2 * TILE]
            sample = jnp.where(
                lane < TILE // 2,
                lanes_at(rows[0:count], off_ref[...]),
                lanes_at(rows[count : 2 * count], off_ref[...]),
            )
            drive = drive + dipole_rows(c) * sample
        return drive * TIME_STEP

    def feed_field(moved):
        for c in range(3):
            sums = lanes_at(moved * dipole_rows(c), perm_ref[...])
            d = 1
            level = 0
            while d < TILE // 2:
                sums = sums + same_ref[level] * shift_lanes(sums, d)
                d *= 2
                level += 1
            rows = [lanes_at(sums, last_ref[k]) * some_ref[k] for k in range(2)]
            parts = jnp.concatenate(split(jnp.concatenate(rows, axis=0)), axis=1)
            change = product(unpick[...], parts)
            change = change[:, 0:TILE] + change[:, TILE : 2 * TILE]
            for h in range(2):
                part = slice(h * TILE, (h + 1) * TILE)
                ep[c, 0:cols, part] = ep[c, 0:cols, part] - change[h * cols : (h + 1) * cols, :]

    def advance(step, start, number):
        def one(i, carry):
            s = start + i
            part = pl.ds(pl.multiple_of(s * TILE, TILE), TILE)
            real = dens[0:pairs, part]
            imag = dens[pairs : 2 * pairs, part]
            force = drive_recv[pl.ds(step * count + s, 1), :]
            out = product(later_ref[...], stacked(real, imag))
            keep = keep_ref[...]
            spacing = spacing_ref[...]
            dens[0:pairs, part] = keep * real + spacing * imag + force * out[0:pairs, TILE:]
            dens[pairs : 2 * pairs, part] = (
                keep * imag - spacing * real - force * out[0:pairs, 0:TILE]
            )
            seen = out[pairs : pairs + 8, 0:TILE] + out[pairs + 8 : pairs + 16, TILE:]
            coef_next[pl.ds(pl.multiple_of(s * 8, 8), 8), :] = seen + force * shift_rows(seen, 4)
            return carry

        lax.fori_loop(0, number, one, 0, unroll=4)

    middle = count // 2

    def one_step(step, carry):
        @pl.when(step >= 2)
        def _():
            advance(step - 2, middle, count - middle)

        @pl.when(step >= 1)
        def _():
            all_drive(step - 1).wait_recv()
            force = drive_recv[pl.ds(pl.multiple_of((step - 1) * count, count), count), :]

            def coef(k):
                return coef_next[pl.ds(k, count, stride=8), :]

            send_coef(step, coef(0) + force * coef(2), coef(1) + force * coef(3))

        e_plane.wait_recv()
        e_row.wait_recv()
        step_h()
        h_row.start()
        h_plane.start()

        @pl.when(step == 0)
        def _():
            find_places()

        @pl.when(step >= 1)
        def _():
            advance(step - 1, 0, middle)

        e_plane.wait_send()
        e_row.wait_send()
        h_plane.wait_recv()
        h_row.wait_recv()
        step_e()

        @pl.when(step == 0)
        def _():
            all_dip.wait_recv()

        drive = sampled_drive()
        drive_send[pl.ds(pl.multiple_of(step * count, count), count), :] = drive
        to_all(
            drive_send,
            drive_recv,
            step * count,
            1,
            1,
            drive_ssem.at[step],
            drive_rsem.at[step],
        )
        h_plane.wait_send()
        h_row.wait_send()
        all_coef(step).wait_recv()
        base = step * 2 * count
        alpha = coef_recv[pl.ds(base, count, stride=2), :]
        beta = coef_recv[pl.ds(base + 1, count, stride=2), :]
        feed_field(alpha + drive * beta)

        @pl.when(step < STEPS - 1)
        def _():
            send_e()

        return carry

    lax.fori_loop(0, STEPS, one_step, 0)

    for copy in field_stores:
        copy.start()
    advance(STEPS - 2, middle, count - middle)
    all_drive(STEPS - 1).wait_recv()

    @pl.loop(0, gx)
    def _(g):
        advance(STEPS - 1, g * gy, gy)
        store_group(g).start()

    all_dip.wait_send()

    @pl.loop(0, STEPS)
    def _(step):
        all_drive(step).wait_send()
        all_coef(step).wait_send()

    for copy in field_stores:
        copy.wait()

    @pl.loop(0, gx)
    def _(g):
        store_group(g).wait()


def body(
    field_e,
    field_h,
    density,
    dipole,
    levels,
    coupling,
    rates,
    tile_cells,
    tile_owner,
    emitter_offsets,
):
    gx = lax.axis_size("gx")
    gy = lax.axis_size("gy")
    count = gx * gy
    _, cx, cy, nz = field_e.shape
    cols = cx * cy
    pairs = coupling.shape[0] ** 2
    columns = density.shape[3]

    vmem = pl.BlockSpec(memory_space=pltpu.VMEM)
    hbm = pl.BlockSpec(memory_space=pl.ANY)
    dma = pltpu.SemaphoreType.DMA
    tall = (count, TILE)
    e_out, h_out, dens_out = pl.pallas_call(
        functools.partial(kernel, gx, gy, cx, cy),
        out_shape=(
            jax.ShapeDtypeStruct((3, cols, nz), F32),
            jax.ShapeDtypeStruct((3, cols, nz), F32),
            jax.ShapeDtypeStruct((2 * pairs, columns), F32),
        ),
        in_specs=[vmem] * 6 + [hbm] * 4,
        out_specs=(hbm, hbm, hbm),
        scratch_shapes=[
            pltpu.VMEM((2 * pairs, columns), F32),
            pltpu.VMEM((3, columns), F32),
            pltpu.VMEM((2 * count, 2 * cols), BF16),
            pltpu.VMEM((2 * cols, 2 * count), BF16),
            pltpu.VMEM(tall, jnp.int32),
            pltpu.VMEM(tall, jnp.int32),
            pltpu.VMEM((2,) + tall, jnp.int32),
            pltpu.VMEM((2,) + tall, F32),
            pltpu.VMEM((6,) + tall, F32),
            pltpu.VMEM((16, 3 * pairs), BF16),
            pltpu.VMEM((pairs + 16, 3 * pairs), BF16),
            pltpu.VMEM((pairs, TILE), F32),
            pltpu.VMEM((pairs, TILE), F32),
            pltpu.VMEM((3, cols + cy, nz), F32),
            pltpu.VMEM((3, cols + cy, nz), F32),
            pltpu.VMEM((2, cx, nz), F32),
            pltpu.VMEM((2, cx, nz), F32),
            pltpu.VMEM((2, cx, nz), F32),
            pltpu.VMEM((2, cx, nz), F32),
            pltpu.VMEM((4 * count, TILE), F32),
            pltpu.VMEM((4 * count, TILE), F32),
            pltpu.VMEM((STEPS * count, TILE), F32),
            pltpu.VMEM((STEPS * count, TILE), F32),
            pltpu.VMEM((STEPS * 2 * count, TILE), F32),
            pltpu.VMEM((STEPS * 2 * count, TILE), F32),
            pltpu.VMEM((8 * count, TILE), F32),
            dma((4,)),
            dma((4,)),
            dma((2,)),
            dma((STEPS,)),
            dma((STEPS,)),
            dma((STEPS,)),
            dma((STEPS,)),
            dma((gx,)),
            dma((gx,)),
            dma((3,)),
        ],
        compiler_params=pltpu.CompilerParams(
            collective_id=0, has_side_effects=True, vmem_limit_bytes=48 * 1024 * 1024
        ),
    )(
        levels.reshape(1, -1),
        coupling,
        rates,
        tile_cells.reshape(1, -1),
        tile_owner.reshape(1, -1),
        emitter_offsets,
        field_e.reshape(3, cols, nz),
        field_h.reshape(3, cols, nz),
        density.reshape(2 * pairs, columns),
        dipole,
    )
    return (
        e_out.reshape(field_e.shape),
        h_out.reshape(field_h.shape),
        dens_out.reshape(density.shape),
    )


def solution(mesh):
    placed = (
        P(None, "gx", "gy", None),
        P(None, "gx", "gy", None),
        P(None, None, None, ("gx", "gy")),
        P(None, ("gx", "gy")),
        P(),
        P(),
        P(),
        P(("gx", "gy")),
        P(("gx", "gy"), None),
        P(("gx", "gy"), None),
    )
    return jax.shard_map(
        body,
        mesh=mesh,
        in_specs=placed,
        out_specs=(
            P(None, "gx", "gy", None),
            P(None, "gx", "gy", None),
            P(None, None, None, ("gx", "gy")),
        ),
        check_vma=False,
    )
```

```python
import functools

import jax
import jax.numpy as jnp
from jax import lax
from jax.experimental import pallas as pl
from jax.experimental.pallas import tpu as pltpu
from jax.sharding import PartitionSpec as P

TILE = 128
STEPS = 4
COURANT = 0.5
TIME_STEP = 0.12
WIDTH = 2
UNROLL = 4

MESH = pl.DeviceIdType.MESH
F32 = jnp.float32
BF16 = jnp.bfloat16


def iota(shape, axis):
    return lax.broadcasted_iota(jnp.int32, shape, axis)


def lanes_at(values, index):
    return jnp.take_along_axis(values, index, axis=1, mode="promise_in_bounds")


def split(values):
    high = values.astype(BF16)
    return high, (values - high.astype(F32)).astype(BF16)


def product(left, right):
    return jnp.dot(left, right, preferred_element_type=F32)


def stacked(real, imag):
    real_high, real_low = split(real)
    imag_high, imag_low = split(imag)
    high = jnp.concatenate([real_high, imag_high], axis=1)
    low = jnp.concatenate([real_low, imag_low], axis=1)
    return jnp.concatenate([high, low, high], axis=0)


def exact(left, right):
    return jnp.dot(left, right, preferred_element_type=F32, precision=lax.Precision.HIGHEST)


def exact_t(left, right):
    return lax.dot_general(
        left,
        right,
        (((1,), (1,)), ((), ())),
        preferred_element_type=F32,
        precision=lax.Precision.HIGHEST,
    )


def shift_rows(values, amount):
    return pltpu.roll(values, amount % values.shape[0], 0)


def shift_lanes(values, amount):
    return pltpu.roll(values, amount % values.shape[1], 1)


def level_constants(levels, coupling, rates, size):
    pairs = size * size
    first = jnp.where(iota((pairs, size), 0) // size == iota((pairs, size), 1), 1.0, 0.0).astype(F32)
    second = jnp.where(iota((pairs, size), 0) % size == iota((pairs, size), 1), 1.0, 0.0).astype(F32)
    row_at, col_at = iota((pairs, pairs), 0), iota((pairs, pairs), 1)
    eye = jnp.where(row_at == col_at, 1.0, 0.0).astype(F32)

    def pair_of(pick):
        half = exact(pick, coupling)
        return 0.5 * (exact_t(half, pick) + exact_t(pick, half))

    def symmetrized(values):
        return 0.5 * (
            jnp.sum(exact(first, values) * second, axis=1, keepdims=True)
            + jnp.sum(exact(second, values) * first, axis=1, keepdims=True)
        )

    def as_row(column):
        return jnp.sum(eye * column, axis=0, keepdims=True)

    commute = jnp.where(row_at % size == col_at % size, pair_of(first), 0.0) - jnp.where(
        row_at // size == col_at // size, pair_of(second), 0.0
    )
    sym = symmetrized(coupling)
    off_diagonal = jnp.where(
        iota((pairs, 1), 0) // size == iota((pairs, 1), 0) % size, 0.0, 1.0
    ).astype(F32)
    decay = TIME_STEP * symmetrized(rates) * off_diagonal
    spacing = TIME_STEP * jnp.sum((first - second) * levels, axis=1, keepdims=True)

    sym_row, decay_row, spacing_row = as_row(sym), as_row(decay), as_row(spacing)
    rows = iota((8, pairs), 0)

    def free(real, imag):
        keep = 1.0 - decay_row
        return real * keep - imag * spacing_row, real * spacing_row + imag * keep

    def driven(real, imag):
        return -exact(imag, commute), exact(real, commute)

    def both(real, imag, distance):
        free_real, free_imag = free(real, imag)
        driven_real, driven_imag = driven(real, imag)
        return (
            free_real + shift_rows(driven_real, distance),
            free_imag + shift_rows(driven_imag, distance),
        )

    push = exact(jnp.broadcast_to(sym_row, (8, pairs)), commute)
    real_zero = jnp.where(rows == 0, -sym_row * decay_row, 0.0)
    imag_zero = jnp.where(rows == 0, sym_row * spacing_row, jnp.where(rows == 1, push, 0.0))
    real_one, imag_one = both(real_zero, imag_zero, 2)
    real_two, imag_two = both(real_one, imag_one, 4)

    def parts(matrix):
        high, low = split(matrix)
        return jnp.concatenate([high, high, low], axis=1)

    begin = parts(
        jnp.concatenate(
            [real_one + shift_rows(real_zero, 4), imag_one + shift_rows(imag_zero, 4)], axis=0
        )
    )
    later = parts(jnp.concatenate([commute, real_two, imag_two], axis=0))
    keep = jnp.broadcast_to(1.0 - decay, (pairs, TILE))
    spacing = jnp.broadcast_to(spacing, (pairs, TILE))
    return begin, later, keep, spacing


def kernel(
    gx,
    gy,
    cx,
    cy,
    levels_hbm,
    coupling_hbm,
    rates_hbm,
    cells_hbm,
    owner_hbm,
    offsets_hbm,
    e_in,
    h_in,
    dens_in,
    dip_in,
    ep,
    hp,
    dens,
    drive_recv,
    later_ref,
    keep_ref,
    spacing_ref,
    levels_in,
    coupling_in,
    rates_in,
    cells_in,
    owner_in,
    offsets_in,
    dip_mine,
    pick,
    unpick,
    off_ref,
    perm_ref,
    last_ref,
    some_ref,
    same_ref,
    begin_ref,
    row_e,
    row_h,
    halo_e,
    halo_h,
    dip_send,
    dip_recv,
    drive_send,
    coef_send,
    coef_recv,
    coef_next,
    halo_send,
    halo_recv,
    dip_sems,
    drive_ssem,
    drive_rsem,
    coef_ssem,
    coef_rsem,
    in_sem,
    small_sem,
    field_sem,
):
    mx = lax.axis_index("gx")
    my = lax.axis_index("gy")
    me = mx * gy + my
    count = gx * gy
    plane = cy
    cols = cx * cy
    nz = 2 * TILE
    group = gy * TILE
    size = levels_in.shape[1]
    pairs = size * size

    def load_group(g):
        part = pl.ds(pl.multiple_of(g * group, group), group)
        return pltpu.make_async_copy(dens_in.at[:, part], dens.at[:, part], in_sem.at[g])

    field_loads = (
        pltpu.make_async_copy(e_in, ep.at[:, 0:cols, :], field_sem.at[0]),
        pltpu.make_async_copy(h_in, hp.at[:, plane : plane + cols, :], field_sem.at[1]),
    )
    small_loads = [
        pltpu.make_async_copy(source, target, small_sem.at[i])
        for i, (source, target) in enumerate(
            (
                (levels_hbm, levels_in),
                (coupling_hbm, coupling_in),
                (rates_hbm, rates_in),
                (cells_hbm, cells_in),
                (owner_hbm, owner_in),
                (offsets_hbm, offsets_in),
            )
        )
    ]
    dip_load = pltpu.make_async_copy(dip_in, dip_mine, field_sem.at[2])

    def along_x(j):
        return lax.rem(mx + j, gx)

    def along_y(j):
        return lax.rem(my + j, gy)

    def device_of(number):
        return number >> (gy.bit_length() - 1), number & (gy - 1)

    def other(j):
        return (me + j) & (count - 1)

    def to_all(source, target, base, step_of, width, send_sem, recv_sem):
        def one(j, carry):
            peer = other(j)
            pltpu.make_async_remote_copy(
                src_ref=source.at[pl.ds(base + peer * step_of, width), :],
                dst_ref=target.at[pl.ds(base + me * step_of, width), :],
                send_sem=send_sem,
                recv_sem=recv_sem,
                device_id=device_of(peer),
                device_id_type=MESH,
            ).start()
            return carry

        lax.fori_loop(1, count, one, 0, unroll=8)
        own = pl.ds(base + me * step_of, width)
        target[own, :] = source[own, :]

    def whole(source, target, base, width, send_sem, recv_sem):
        rows = pl.ds(base, (count - 1) * width)
        return pltpu.make_async_remote_copy(
            src_ref=source.at[rows, :],
            dst_ref=target.at[rows, :],
            send_sem=send_sem,
            recv_sem=recv_sem,
            device_id=(along_x(1), my),
            device_id_type=MESH,
        )

    def all_drive(step):
        return whole(
            drive_send, drive_recv, step * count, 1, drive_ssem.at[step], drive_rsem.at[step]
        )

    def all_coef(step):
        return whole(
            coef_send, coef_recv, step * 2 * count, 2, coef_ssem.at[step], coef_rsem.at[step]
        )

    all_dip = whole(dip_send, dip_recv, 0, 4, dip_sems.at[0], dip_sems.at[1])

    x_below, x_above = along_x(gx - 1), along_x(1)
    y_below, y_above = along_y(gy - 1), along_y(1)

    def halo_copy(which, source, target, device):
        return pltpu.make_async_remote_copy(
            src_ref=source,
            dst_ref=target,
            send_sem=halo_send.at[which],
            recv_sem=halo_recv.at[which],
            device_id=device,
            device_id_type=MESH,
        )

    e_plane = halo_copy(
        0, ep.at[1:3, 0:plane, :], ep.at[1:3, cols : cols + plane, :], (x_below, my)
    )
    e_row = halo_copy(1, row_e, halo_e, (mx, y_below))
    h_plane = halo_copy(
        2, hp.at[1:3, cols : cols + plane, :], hp.at[1:3, 0:plane, :], (x_above, my)
    )
    h_row = halo_copy(3, row_h, halo_h, (mx, y_above))

    def send_e():
        for x in range(cx):
            row_e[0, x : x + 1, :] = ep[0, x * plane : x * plane + 1, :]
            row_e[1, x : x + 1, :] = ep[2, x * plane : x * plane + 1, :]
        e_row.start()
        e_plane.start()

    for copy in small_loads:
        copy.start()
    dip_load.start()
    for copy in field_loads:
        copy.start()

    @pl.loop(0, gx)
    def _(g):
        load_group(g).start()

    barrier = pltpu.get_barrier_semaphore()

    def greet(j, carry):
        pl.semaphore_signal(barrier, inc=1, device_id=device_of(other(j)), device_id_type=MESH)
        return carry

    lax.fori_loop(1, count, greet, 0, unroll=8)

    for copy in small_loads:
        copy.wait()
    begin, later, keep, spacing = level_constants(
        levels_in[...], coupling_in[...], rates_in[...], size
    )
    begin_ref[...] = begin
    later_ref[...] = later
    keep_ref[...] = keep
    spacing_ref[...] = spacing

    dip_load.wait()

    def dip_row(s, carry):
        lanes = pl.ds(pl.multiple_of(s * TILE, TILE), TILE)
        dip_send[pl.ds(pl.multiple_of(s * 4, 4), 3), :] = dip_mine[:, lanes]
        return carry

    dip_send[pl.ds(3, count, stride=4), :] = jnp.zeros((count, TILE), F32)
    lax.fori_loop(0, count, dip_row, 0, unroll=8)
    for copy in field_loads:
        copy.wait()

    pl.semaphore_wait(barrier, count - 1)
    send_e()
    to_all(dip_send, dip_recv, 0, 4, 4, dip_sems.at[0], dip_sems.at[1])

    def look_first():
        @pl.loop(0, gx)
        def _(g):
            load_group(g).wait()

        def one(s, carry):
            part = pl.ds(pl.multiple_of(s * TILE, TILE), TILE)
            state = stacked(dens[0:pairs, part], dens[pairs : 2 * pairs, part])
            seen = product(begin_ref[...], state)
            coef_next[pl.ds(pl.multiple_of(s * 8, 8), 8), :] = seen[0:8, 0:TILE] + seen[8:16, TILE:]
            return carry

        lax.fori_loop(0, count, one, 0, unroll=4)

    def send_coef(step, alpha, beta):
        base = step * 2 * count
        coef_send[pl.ds(base, count, stride=2), :] = alpha
        coef_send[pl.ds(base + 1, count, stride=2), :] = beta
        to_all(coef_send, coef_recv, base, 2, 2, coef_ssem.at[step], coef_rsem.at[step])

    lane = iota((count, TILE), 1)
    sub = iota((count, TILE), 0)

    def find_places():
        eye = jnp.where(lane == sub, 1.0, 0.0).astype(F32)

        def column_of(row):
            return jnp.sum(eye * row, axis=1, keepdims=True)

        owner_row = owner_in[...].astype(F32)
        owner_col = column_of(owner_row)
        tiles = cells_in[...]
        cell_row = ((tiles & 1) * cols + (tiles >> 1)).astype(F32)
        cell_col = column_of(cell_row)
        alike = jnp.where(owner_col == owner_row, 1.0, 0.0)
        rank_col = jnp.sum(jnp.where(lane < sub, alike, 0.0), axis=1, keepdims=True)
        rank_row = jnp.sum(jnp.where(sub < lane, alike, 0.0), axis=0, keepdims=True)

        def flags(condition):
            return jnp.where(condition, 1.0, 0.0).astype(BF16)

        named = owner_row == sub.astype(F32)
        slot_zero = flags(named & (rank_row == 0.0))
        slot_one = flags(named & (rank_row == 1.0))
        taking = owner_col == lane.astype(F32)
        slot_zero_t = flags(taking & (rank_col == 0.0))
        slot_one_t = flags(taking & (rank_col == 1.0))
        at_cell = flags(cell_col == iota((count, 2 * cols), 1).astype(F32))
        at_cell_t = flags(cell_row == iota((2 * cols, count), 0).astype(F32))
        pick[0:count, :] = product(slot_zero, at_cell).astype(BF16)
        pick[count : 2 * count, :] = product(slot_one, at_cell).astype(BF16)
        unpick[:, 0:count] = product(at_cell_t, slot_zero_t).astype(BF16)
        unpick[:, count : 2 * count] = product(at_cell_t, slot_one_t).astype(BF16)

        offsets = offsets_in[...].astype(F32).astype(BF16)

        def offsets_of(slot):
            return lax.dot_general(
                slot, offsets, (((1,), (1,)), ((), ())), preferred_element_type=F32
            )

        off = jnp.concatenate([offsets_of(slot_zero), offsets_of(slot_one)], axis=1)
        off = off.astype(jnp.int32)
        off_ref[...] = off

        half = TILE // 2
        place = lane & (half - 1)
        base = lane & half
        key = off * half + place
        length = 2
        while length <= half:
            d = length // 2
            while d >= 1:
                partner = lanes_at(key, lane ^ d)
                lower = jnp.where((lane & d) == 0, 1, 0)
                upward = jnp.where((place & length) == 0, 1, 0)
                key = jnp.where(
                    lower == upward, jnp.minimum(key, partner), jnp.maximum(key, partner)
                )
                d //= 2
            length *= 2
        perm_ref[...] = base | (key & (half - 1))
        ordered = key >> 6
        d = 1
        level = 0
        while d < half:
            together = (place >= d) & (shift_lanes(ordered, d) == ordered)
            same_ref[level] = jnp.where(together, 1.0, 0.0).astype(F32)
            d *= 2
            level += 1
        for k in range(2):
            found = jnp.zeros((count, TILE), jnp.int32)
            jump = half // 2
            while jump >= 1:
                seen = lanes_at(ordered, found + (k * half + jump - 1))
                found = jnp.where(seen <= lane, found + jump, found)
                jump //= 2
            seen = lanes_at(ordered, found + k * half)
            found = jnp.where(seen <= lane, found + 1, found)
            last = jnp.maximum(found - 1, 0) + k * half
            hit = (found > 0) & (lanes_at(ordered, last) == lane)
            last_ref[k] = last
            some_ref[k] = jnp.where(hit, 1.0, 0.0).astype(F32)

    row_at = iota((plane, nz), 0)
    z_at = iota((plane, nz), 1)

    def next_y(values, row):
        return jnp.where(row_at == plane - 1, row, shift_rows(values, -1))

    def prior_y(values, row):
        return jnp.where(row_at == 0, row, shift_rows(values, 1))

    def next_z(values):
        return jnp.where(z_at == nz - 1, 0.0, shift_lanes(values, -1))

    def prior_z(values):
        return jnp.where(z_at == 0, 0.0, shift_lanes(values, 1))

    def step_h():
        keep_x = jnp.where(mx == gx - 1, 0.0, 1.0).astype(F32)
        keep_y = jnp.where(my == gy - 1, 0.0, 1.0).astype(F32)
        for c in (1, 2):
            ep[c, cols : cols + plane, :] = ep[c, cols : cols + plane, :] * keep_x
        for x in range(cx):
            here = slice(x * plane, (x + 1) * plane)
            after = slice((x + 1) * plane, (x + 2) * plane)
            e0, e1, e2 = ep[0, here, :], ep[1, here, :], ep[2, here, :]
            e1_x, e2_x = ep[1, after, :], ep[2, after, :]
            e0_y = next_y(e0, halo_e[0, x : x + 1, :] * keep_y)
            e2_y = next_y(e2, halo_e[1, x : x + 1, :] * keep_y)
            hp[0, after, :] = hp[0, after, :] - COURANT * ((e2_y - e2) - (next_z(e1) - e1))
            hp[1, after, :] = hp[1, after, :] - COURANT * ((next_z(e0) - e0) - (e2_x - e2))
            hp[2, after, :] = hp[2, after, :] - COURANT * ((e1_x - e1) - (e0_y - e0))
            bottom = slice((x + 2) * plane - 1, (x + 2) * plane)
            row_h[0, x : x + 1, :] = hp[0, bottom, :]
            row_h[1, x : x + 1, :] = hp[2, bottom, :]

    def step_e():
        hold_x = jnp.where(mx == 0, 0.0, 1.0).astype(F32)
        hold_y = jnp.where(my == 0, 0.0, 1.0).astype(F32)
        for c in (1, 2):
            hp[c, 0:plane, :] = hp[c, 0:plane, :] * hold_x
        for x in range(cx):
            here = slice(x * plane, (x + 1) * plane)
            after = slice((x + 1) * plane, (x + 2) * plane)
            h0, h1, h2 = hp[0, after, :], hp[1, after, :], hp[2, after, :]
            h1_x, h2_x = hp[1, here, :], hp[2, here, :]
            h0_y = prior_y(h0, halo_h[0, x : x + 1, :] * hold_y)
            h2_y = prior_y(h2, halo_h[1, x : x + 1, :] * hold_y)
            ep[0, here, :] = ep[0, here, :] + COURANT * ((h2 - h2_y) - (h1 - prior_z(h1)))
            ep[1, here, :] = ep[1, here, :] + COURANT * ((h0 - prior_z(h0)) - (h2 - h2_x))
            ep[2, here, :] = ep[2, here, :] + COURANT * ((h1 - h1_x) - (h0 - h0_y))

    def dipole_rows(c):
        return dip_recv[pl.ds(c, count, stride=4), :]

    def sampled_drive():
        drive = jnp.zeros((count, TILE), F32)
        for c in range(3):
            rows = jnp.zeros((2 * count, 2 * TILE), F32)
            for h in range(2):
                parts = jnp.concatenate(split(ep[c, 0:cols, h * TILE : (h + 1) * TILE]), axis=1)
                rows = rows + product(pick[:, h * cols : (h + 1) * cols], parts)
            rows = rows[:, 0:TILE] + rows[:, TILE : 2 * TILE]
            sample = jnp.where(
                lane < TILE // 2,
                lanes_at(rows[0:count], off_ref[...]),
                lanes_at(rows[count : 2 * count], off_ref[...]),
            )
            drive = drive + dipole_rows(c) * sample
        return drive * TIME_STEP

    def feed_field(moved):
        for c in range(3):
            sums = lanes_at(moved * dipole_rows(c), perm_ref[...])
            d = 1
            level = 0
            while d < TILE // 2:
                sums = sums + same_ref[level] * shift_lanes(sums, d)
                d *= 2
                level += 1
            rows = [lanes_at(sums, last_ref[k]) * some_ref[k] for k in range(2)]
            parts = jnp.concatenate(split(jnp.concatenate(rows, axis=0)), axis=1)
            change = product(unpick[...], parts)
            change = change[:, 0:TILE] + change[:, TILE : 2 * TILE]
            for h in range(2):
                part = slice(h * TILE, (h + 1) * TILE)
                ep[c, 0:cols, part] = ep[c, 0:cols, part] - change[h * cols : (h + 1) * cols, :]

    def advance(step, start, number):
        def look(g):
            part = pl.ds(pl.multiple_of((start + WIDTH * g) * TILE, WIDTH * TILE), WIDTH * TILE)
            return product(
                later_ref[...], stacked(dens[0:pairs, part], dens[pairs : 2 * pairs, part])
            )

        rounds = number // WIDTH

        def one(g, out):
            after = look(jnp.minimum(g + 1, rounds - 1))
            keep = keep_ref[...]
            spacing = spacing_ref[...]
            for w in range(WIDTH):
                s = start + WIDTH * g + w
                part = pl.ds(pl.multiple_of(s * TILE, TILE), TILE)
                left = slice(w * TILE, (w + 1) * TILE)
                right = slice((WIDTH + w) * TILE, (WIDTH + w + 1) * TILE)
                real = dens[0:pairs, part]
                imag = dens[pairs : 2 * pairs, part]
                force = drive_recv[pl.ds(step * count + s, 1), :]
                dens[0:pairs, part] = keep * real + spacing * imag + force * out[0:pairs, right]
                dens[pairs : 2 * pairs, part] = (
                    keep * imag - spacing * real - force * out[0:pairs, left]
                )
                seen = out[pairs : pairs + 8, left] + out[pairs + 8 : pairs + 16, right]
                coef_next[pl.ds(pl.multiple_of(s * 8, 8), 8), :] = seen + force * shift_rows(
                    seen, 4
                )
            return after

        lax.fori_loop(0, rounds, one, look(0), unroll=UNROLL)

    middle = count // 2

    def one_step(step, carry):
        @pl.when(step >= 2)
        def _():
            advance(step - 2, middle, count - middle)

        @pl.when(step >= 1)
        def _():
            all_drive(step - 1).wait_recv()
            force = drive_recv[pl.ds(pl.multiple_of((step - 1) * count, count), count), :]

            def coef(k):
                return coef_next[pl.ds(k, count, stride=8), :]

            send_coef(step, coef(0) + force * coef(2), coef(1) + force * coef(3))

        e_plane.wait_recv()
        e_row.wait_recv()
        step_h()
        h_row.start()
        h_plane.start()

        @pl.when(step == 0)
        def _():
            look_first()
            send_coef(
                0,
                coef_next[pl.ds(4, count, stride=8), :],
                coef_next[pl.ds(5, count, stride=8), :],
            )

        @pl.when(step >= 1)
        def _():
            advance(step - 1, 0, middle)

        e_plane.wait_send()
        e_row.wait_send()
        h_plane.wait_recv()
        h_row.wait_recv()
        step_e()

        @pl.when(step == 0)
        def _():
            all_dip.wait_recv()

        drive = sampled_drive()
        drive_send[pl.ds(pl.multiple_of(step * count, count), count), :] = drive
        to_all(
            drive_send,
            drive_recv,
            step * count,
            1,
            1,
            drive_ssem.at[step],
            drive_rsem.at[step],
        )
        h_plane.wait_send()
        h_row.wait_send()
        all_coef(step).wait_recv()
        base = step * 2 * count
        alpha = coef_recv[pl.ds(base, count, stride=2), :]
        beta = coef_recv[pl.ds(base + 1, count, stride=2), :]
        feed_field(alpha + drive * beta)

        @pl.when(step < STEPS - 1)
        def _():
            send_e()

        return carry

    find_places()
    lax.fori_loop(0, STEPS, one_step, 0)

    advance(STEPS - 2, middle, count - middle)
    all_drive(STEPS - 1).wait_recv()
    all_dip.wait_send()

    @pl.loop(0, STEPS)
    def _(step):
        all_drive(step).wait_send()
        all_coef(step).wait_send()


def finish(
    gx,
    gy,
    plane,
    ep,
    hp,
    dens,
    drive_recv,
    later_ref,
    keep_ref,
    spacing_ref,
    e_out,
    h_out,
    dens_out,
    fresh,
    out_sem,
    field_sem,
):
    count = gx * gy
    cols = e_out.shape[1]
    pairs = dens.shape[0] // 2
    group = gy * TILE
    wide = WIDTH * TILE
    field_stores = (
        pltpu.make_async_copy(ep.at[:, 0:cols, :], e_out, field_sem.at[0]),
        pltpu.make_async_copy(hp.at[:, plane : plane + cols, :], h_out, field_sem.at[1]),
    )
    for copy in field_stores:
        copy.start()

    def store_group(g):
        part = pl.ds(pl.multiple_of(g * group, group), group)
        return pltpu.make_async_copy(fresh.at[:, part], dens_out.at[:, part], out_sem.at[g])

    def look(g):
        part = pl.ds(pl.multiple_of(g * wide, wide), wide)
        return product(
            later_ref[0:pairs, :], stacked(dens[0:pairs, part], dens[pairs : 2 * pairs, part])
        )

    rounds = count // WIDTH
    per_group = gy // WIDTH

    def one_group(group_at, out):
        for i in range(per_group):
            g = group_at * per_group + i
            after = look(jnp.minimum(g + 1, rounds - 1))
            keep = keep_ref[...]
            spacing = spacing_ref[...]
            for w in range(WIDTH):
                s = WIDTH * g + w
                part = pl.ds(pl.multiple_of(s * TILE, TILE), TILE)
                left = slice(w * TILE, (w + 1) * TILE)
                right = slice((WIDTH + w) * TILE, (WIDTH + w + 1) * TILE)
                real = dens[0:pairs, part]
                imag = dens[pairs : 2 * pairs, part]
                force = drive_recv[pl.ds((STEPS - 1) * count + s, 1), :]
                fresh[0:pairs, part] = keep * real + spacing * imag + force * out[:, right]
                fresh[pairs : 2 * pairs, part] = (
                    keep * imag - spacing * real - force * out[:, left]
                )
            out = after
        store_group(group_at).start()
        return out

    lax.fori_loop(0, gx, one_group, look(0))
    for copy in field_stores:
        copy.wait()

    @pl.loop(0, gx)
    def _(g):
        store_group(g).wait()


def body(
    field_e,
    field_h,
    density,
    dipole,
    levels,
    coupling,
    rates,
    tile_cells,
    tile_owner,
    emitter_offsets,
):
    gx = lax.axis_size("gx")
    gy = lax.axis_size("gy")
    count = gx * gy
    _, cx, cy, nz = field_e.shape
    cols = cx * cy
    pairs = coupling.shape[0] ** 2
    columns = density.shape[3]

    size = coupling.shape[0]
    vmem = pl.BlockSpec(memory_space=pltpu.VMEM)
    hbm = pl.BlockSpec(memory_space=pltpu.HBM)
    dma = pltpu.SemaphoreType.DMA
    tall = (count, TILE)
    padded = jax.ShapeDtypeStruct((3, cols + cy, nz), F32)
    state = pl.pallas_call(
        functools.partial(kernel, gx, gy, cx, cy),
        out_shape=(
            padded,
            padded,
            jax.ShapeDtypeStruct((2 * pairs, columns), F32),
            jax.ShapeDtypeStruct((STEPS * count, TILE), F32),
            jax.ShapeDtypeStruct((pairs + 16, 3 * pairs), BF16),
            jax.ShapeDtypeStruct((pairs, TILE), F32),
            jax.ShapeDtypeStruct((pairs, TILE), F32),
        ),
        in_specs=[hbm] * 10,
        out_specs=(vmem,) * 7,
        scratch_shapes=[
            pltpu.VMEM((1, size), F32),
            pltpu.VMEM((size, size), F32),
            pltpu.VMEM((size, size), F32),
            pltpu.VMEM((1, count), jnp.int32),
            pltpu.VMEM((1, count), jnp.int32),
            pltpu.VMEM((TILE // 2, count), jnp.int32),
            pltpu.VMEM((3, columns), F32),
            pltpu.VMEM((2 * count, 2 * cols), BF16),
            pltpu.VMEM((2 * cols, 2 * count), BF16),
            pltpu.VMEM(tall, jnp.int32),
            pltpu.VMEM(tall, jnp.int32),
            pltpu.VMEM((2,) + tall, jnp.int32),
            pltpu.VMEM((2,) + tall, F32),
            pltpu.VMEM((6,) + tall, F32),
            pltpu.VMEM((16, 3 * pairs), BF16),
            pltpu.VMEM((2, cx, nz), F32),
            pltpu.VMEM((2, cx, nz), F32),
            pltpu.VMEM((2, cx, nz), F32),
            pltpu.VMEM((2, cx, nz), F32),
            pltpu.VMEM((4 * count, TILE), F32),
            pltpu.VMEM((4 * count, TILE), F32),
            pltpu.VMEM((STEPS * count, TILE), F32),
            pltpu.VMEM((STEPS * 2 * count, TILE), F32),
            pltpu.VMEM((STEPS * 2 * count, TILE), F32),
            pltpu.VMEM((8 * count, TILE), F32),
            dma((4,)),
            dma((4,)),
            dma((2,)),
            dma((STEPS,)),
            dma((STEPS,)),
            dma((STEPS,)),
            dma((STEPS,)),
            dma((gx,)),
            dma((6,)),
            dma((3,)),
        ],
        compiler_params=pltpu.CompilerParams(
            collective_id=0, has_side_effects=True, vmem_limit_bytes=24 * 1024 * 1024
        ),
    )(*(pltpu.with_memory_space_constraint(x, pltpu.HBM) for x in (
        levels.reshape(1, -1),
        coupling,
        rates,
        tile_cells.reshape(1, -1),
        tile_owner.reshape(1, -1),
        emitter_offsets.T,
        field_e.reshape(3, cols, nz),
        field_h.reshape(3, cols, nz),
        density.reshape(2 * pairs, columns),
        dipole,
    )))
    e_out, h_out, dens_out = pl.pallas_call(
        functools.partial(finish, gx, gy, cy),
        out_shape=(
            jax.ShapeDtypeStruct((3, cols, nz), F32),
            jax.ShapeDtypeStruct((3, cols, nz), F32),
            jax.ShapeDtypeStruct((2 * pairs, columns), F32),
        ),
        in_specs=[vmem] * 7,
        out_specs=(hbm, hbm, hbm),
        scratch_shapes=[
            pltpu.VMEM((2 * pairs, columns), F32),
            dma((gx,)),
            dma((2,)),
        ],
        compiler_params=pltpu.CompilerParams(vmem_limit_bytes=24 * 1024 * 1024),
    )(*state)
    return (
        e_out.reshape(field_e.shape),
        h_out.reshape(field_h.shape),
        dens_out.reshape(density.shape),
    )


def solution(mesh):
    placed = (
        P(None, "gx", "gy", None),
        P(None, "gx", "gy", None),
        P(None, None, None, ("gx", "gy")),
        P(None, ("gx", "gy")),
        P(),
        P(),
        P(),
        P(("gx", "gy")),
        P(("gx", "gy"), None),
        P(("gx", "gy"), None),
    )
    return jax.shard_map(
        body,
        mesh=mesh,
        in_specs=placed,
        out_specs=(
            P(None, "gx", "gy", None),
            P(None, "gx", "gy", None),
            P(None, None, None, ("gx", "gy")),
        ),
        check_vma=False,
    )
```

```python
import functools

import jax
import jax.numpy as jnp
from jax import lax
from jax.experimental import pallas as pl
from jax.experimental.pallas import tpu as pltpu
from jax.sharding import PartitionSpec as P

TILE = 128
STEPS = 4
COURANT = 0.5
TIME_STEP = 0.12
WIDTH = 2
FIRST = 4
UNROLL = 4

MESH = pl.DeviceIdType.MESH
F32 = jnp.float32
BF16 = jnp.bfloat16


def iota(shape, axis):
    return lax.broadcasted_iota(jnp.int32, shape, axis)


def lanes_at(values, index):
    return jnp.take_along_axis(values, index, axis=1, mode="promise_in_bounds")


def split(values):
    high = values.astype(BF16)
    return high, (values - high.astype(F32)).astype(BF16)


def product(left, right):
    return jnp.dot(left, right, preferred_element_type=F32)


def stacked(real, imag):
    real_high, real_low = split(real)
    imag_high, imag_low = split(imag)
    high = jnp.concatenate([real_high, imag_high], axis=1)
    low = jnp.concatenate([real_low, imag_low], axis=1)
    return jnp.concatenate([high, low, high], axis=0)


def exact(left, right):
    return jnp.dot(left, right, preferred_element_type=F32, precision=lax.Precision.HIGHEST)


def exact_t(left, right):
    return lax.dot_general(
        left,
        right,
        (((1,), (1,)), ((), ())),
        preferred_element_type=F32,
        precision=lax.Precision.HIGHEST,
    )


def shift_rows(values, amount):
    return pltpu.roll(values, amount % values.shape[0], 0)


def shift_lanes(values, amount):
    return pltpu.roll(values, amount % values.shape[1], 1)


def level_constants(levels, coupling, rates, size):
    pairs = size * size
    first = jnp.where(iota((pairs, size), 0) // size == iota((pairs, size), 1), 1.0, 0.0).astype(F32)
    second = jnp.where(iota((pairs, size), 0) % size == iota((pairs, size), 1), 1.0, 0.0).astype(F32)
    row_at, col_at = iota((pairs, pairs), 0), iota((pairs, pairs), 1)
    eye = jnp.where(row_at == col_at, 1.0, 0.0).astype(F32)

    def pair_of(pick):
        half = exact(pick, coupling)
        return 0.5 * (exact_t(half, pick) + exact_t(pick, half))

    def symmetrized(values):
        return 0.5 * (
            jnp.sum(exact(first, values) * second, axis=1, keepdims=True)
            + jnp.sum(exact(second, values) * first, axis=1, keepdims=True)
        )

    def as_row(column):
        return jnp.sum(eye * column, axis=0, keepdims=True)

    commute = jnp.where(row_at % size == col_at % size, pair_of(first), 0.0) - jnp.where(
        row_at // size == col_at // size, pair_of(second), 0.0
    )
    sym = symmetrized(coupling)
    off_diagonal = jnp.where(
        iota((pairs, 1), 0) // size == iota((pairs, 1), 0) % size, 0.0, 1.0
    ).astype(F32)
    decay = TIME_STEP * symmetrized(rates) * off_diagonal
    spacing = TIME_STEP * jnp.sum((first - second) * levels, axis=1, keepdims=True)

    sym_row, decay_row, spacing_row = as_row(sym), as_row(decay), as_row(spacing)
    rows = iota((16, pairs), 0)

    def free(real, imag):
        keep = 1.0 - decay_row
        return real * keep - imag * spacing_row, real * spacing_row + imag * keep

    def driven(real, imag):
        return -exact(imag, commute), exact(real, commute)

    def both(real, imag, distance):
        free_real, free_imag = free(real, imag)
        driven_real, driven_imag = driven(real, imag)
        return (
            free_real + shift_rows(driven_real, distance),
            free_imag + shift_rows(driven_imag, distance),
        )

    push = exact(jnp.broadcast_to(sym_row, (16, pairs)), commute)
    real_zero = jnp.where(rows == 0, -sym_row * decay_row, 0.0)
    imag_zero = jnp.where(rows == 0, sym_row * spacing_row, jnp.where(rows == 1, push, 0.0))
    real_one, imag_one = both(real_zero, imag_zero, 2)
    real_two, imag_two = both(real_one, imag_one, 4)
    real_three, imag_three = both(real_two, imag_two, 8)

    def parts(matrix):
        high, low = split(matrix)
        return jnp.concatenate([high, high, low], axis=1)

    def opening(zero, one, two):
        return one + shift_rows(zero, 4) + shift_rows(two, 8)

    begin = parts(
        jnp.concatenate(
            [opening(real_zero, real_one, real_two), opening(imag_zero, imag_one, imag_two)],
            axis=0,
        )
    )
    later = parts(jnp.concatenate([commute, real_three, imag_three], axis=0))
    keep = jnp.broadcast_to(1.0 - decay, (pairs, TILE))
    spacing = jnp.broadcast_to(spacing, (pairs, TILE))
    return begin, later, keep, spacing


def kernel(
    gx,
    gy,
    cx,
    cy,
    levels_hbm,
    coupling_hbm,
    rates_hbm,
    cells_hbm,
    owner_hbm,
    offsets_hbm,
    e_in,
    h_in,
    dens_in,
    dip_in,
    ep,
    hp,
    dens,
    drive_recv,
    later_ref,
    keep_ref,
    spacing_ref,
    levels_in,
    coupling_in,
    rates_in,
    cells_in,
    owner_in,
    offsets_in,
    dip_mine,
    pick,
    unpick,
    off_ref,
    perm_ref,
    last_ref,
    some_ref,
    same_ref,
    begin_ref,
    row_e,
    row_h,
    halo_e,
    halo_h,
    dip_send,
    dip_recv,
    drive_send,
    coef0_send,
    coef0_recv,
    coef1_send,
    coef1_recv,
    coef2_send,
    coef2_recv,
    coef3_send,
    coef3_recv,
    looked,
    ahead,
    halo_send,
    halo_recv,
    dip_sems,
    drive_ssem,
    drive_rsem,
    coef_ssem,
    coef_rsem,
    in_sem,
    small_sem,
    field_sem,
):
    mx = lax.axis_index("gx")
    my = lax.axis_index("gy")
    me = mx * gy + my
    count = gx * gy
    plane = cy
    cols = cx * cy
    nz = 2 * TILE
    group = gy * TILE
    size = levels_in.shape[1]
    pairs = size * size

    def load_group(g):
        part = pl.ds(pl.multiple_of(g * group, group), group)
        return pltpu.make_async_copy(dens_in.at[:, part], dens.at[:, part], in_sem.at[g])

    field_loads = (
        pltpu.make_async_copy(e_in, ep.at[:, 0:cols, :], field_sem.at[0]),
        pltpu.make_async_copy(h_in, hp.at[:, plane : plane + cols, :], field_sem.at[1]),
    )
    small_loads = [
        pltpu.make_async_copy(source, target, small_sem.at[i])
        for i, (source, target) in enumerate(
            (
                (levels_hbm, levels_in),
                (coupling_hbm, coupling_in),
                (rates_hbm, rates_in),
                (cells_hbm, cells_in),
                (owner_hbm, owner_in),
                (offsets_hbm, offsets_in),
            )
        )
    ]
    dip_load = pltpu.make_async_copy(dip_in, dip_mine, field_sem.at[2])

    def along_x(j):
        return lax.rem(mx + j, gx)

    def along_y(j):
        return lax.rem(my + j, gy)

    def device_of(number):
        return number >> (gy.bit_length() - 1), number & (gy - 1)

    def other(j):
        return (me + j) & (count - 1)

    def to_all(source, target, base, step_of, width, send_sem, recv_sem):
        def one(j, carry):
            peer = other(j)
            pltpu.make_async_remote_copy(
                src_ref=source.at[pl.ds(base + peer * step_of, width), :],
                dst_ref=target.at[pl.ds(base + me * step_of, width), :],
                send_sem=send_sem,
                recv_sem=recv_sem,
                device_id=device_of(peer),
                device_id_type=MESH,
            ).start()
            return carry

        lax.fori_loop(1, count, one, 0, unroll=8)
        own = pl.ds(base + me * step_of, width)
        target[own, :] = source[own, :]

    def whole(source, target, base, width, send_sem, recv_sem):
        rows = pl.ds(base, (count - 1) * width)
        return pltpu.make_async_remote_copy(
            src_ref=source.at[rows, :],
            dst_ref=target.at[rows, :],
            send_sem=send_sem,
            recv_sem=recv_sem,
            device_id=(along_x(1), my),
            device_id_type=MESH,
        )

    drive_sems = [(drive_ssem.at[step], drive_rsem.at[step]) for step in range(STEPS)]
    coefs = [
        (send, recv, width, coef_ssem.at[step], coef_rsem.at[step])
        for step, (send, recv, width) in enumerate(
            (
                (coef0_send, coef0_recv, 2),
                (coef1_send, coef1_recv, 4),
                (coef2_send, coef2_recv, 4),
                (coef3_send, coef3_recv, 4),
            )
        )
    ]

    def all_drive(step):
        return whole(drive_send, drive_recv, step * count, 1, *drive_sems[step])

    def send_drive(step):
        to_all(drive_send, drive_recv, step * count, 1, 1, *drive_sems[step])

    def all_coef(step):
        send, recv, width, out_sem, back_sem = coefs[step]
        return whole(send, recv, 0, width, out_sem, back_sem)

    def send_coef(step):
        send, recv, width, out_sem, back_sem = coefs[step]
        to_all(send, recv, 0, width, width, out_sem, back_sem)

    all_dip = whole(dip_send, dip_recv, 0, 4, dip_sems.at[0], dip_sems.at[1])

    x_below, x_above = along_x(gx - 1), along_x(1)
    y_below, y_above = along_y(gy - 1), along_y(1)

    def halo_copy(which, source, target, device):
        return pltpu.make_async_remote_copy(
            src_ref=source,
            dst_ref=target,
            send_sem=halo_send.at[which],
            recv_sem=halo_recv.at[which],
            device_id=device,
            device_id_type=MESH,
        )

    e_plane = halo_copy(
        0, ep.at[1:3, 0:plane, :], ep.at[1:3, cols : cols + plane, :], (x_below, my)
    )
    e_row = halo_copy(1, row_e, halo_e, (mx, y_below))
    h_plane = halo_copy(
        2, hp.at[1:3, cols : cols + plane, :], hp.at[1:3, 0:plane, :], (x_above, my)
    )
    h_row = halo_copy(3, row_h, halo_h, (mx, y_above))

    def send_e():
        for x in range(cx):
            row_e[0, x : x + 1, :] = ep[0, x * plane : x * plane + 1, :]
            row_e[1, x : x + 1, :] = ep[2, x * plane : x * plane + 1, :]
        e_row.start()
        e_plane.start()

    for copy in small_loads:
        copy.start()
    dip_load.start()
    for copy in field_loads:
        copy.start()

    @pl.loop(0, gx)
    def _(g):
        load_group(g).start()

    barrier = pltpu.get_barrier_semaphore()

    def greet(j, carry):
        pl.semaphore_signal(barrier, inc=1, device_id=device_of(other(j)), device_id_type=MESH)
        return carry

    lax.fori_loop(1, count, greet, 0, unroll=8)

    for copy in small_loads:
        copy.wait()
    begin, later, keep, spacing = level_constants(
        levels_in[...], coupling_in[...], rates_in[...], size
    )
    begin_ref[...] = begin
    later_ref[...] = later
    keep_ref[...] = keep
    spacing_ref[...] = spacing

    dip_load.wait()

    def dip_row(s, carry):
        lanes = pl.ds(pl.multiple_of(s * TILE, TILE), TILE)
        dip_send[pl.ds(pl.multiple_of(s * 4, 4), 3), :] = dip_mine[:, lanes]
        return carry

    dip_send[pl.ds(3, count, stride=4), :] = jnp.zeros((count, TILE), F32)
    lax.fori_loop(0, count, dip_row, 0, unroll=8)
    for copy in field_loads:
        copy.wait()

    pl.semaphore_wait(barrier, count - 1)
    send_e()
    to_all(dip_send, dip_recv, 0, 4, 4, dip_sems.at[0], dip_sems.at[1])

    def look_first():
        @pl.loop(0, gx)
        def _(g):
            load_group(g).wait()

        def one(g, carry):
            part = pl.ds(pl.multiple_of(g * FIRST * TILE, FIRST * TILE), FIRST * TILE)
            state = stacked(dens[0:pairs, part], dens[pairs : 2 * pairs, part])
            seen = product(begin_ref[...], state)
            seen = seen[0:16, 0 : FIRST * TILE] + seen[16:32, FIRST * TILE :]
            for w in range(FIRST):
                rows = pl.ds(pl.multiple_of((g * FIRST + w) * 16, 16), 16)
                looked[rows, :] = seen[:, w * TILE : (w + 1) * TILE]
            return carry

        lax.fori_loop(0, count // FIRST, one, 0, unroll=4)
        for k in range(4):
            coef1_send[pl.ds(k, count, stride=4), :] = looked[pl.ds(k, count, stride=16), :]
        for k in range(2):
            coef0_send[pl.ds(k, count, stride=2), :] = looked[pl.ds(4 + k, count, stride=16), :]

    def combine(target, source, first, stride, step):
        force = drive_recv[step * count : (step + 1) * count, :]
        for k in range(4):
            target[pl.ds(k, count, stride=4), :] = (
                source[pl.ds(first + k, count, stride=stride), :]
                + force * source[pl.ds(first + k + 4, count, stride=stride), :]
            )

    lane = iota((count, TILE), 1)
    sub = iota((count, TILE), 0)

    def find_places():
        eye = jnp.where(lane == sub, 1.0, 0.0).astype(F32)

        def column_of(row):
            return jnp.sum(eye * row, axis=1, keepdims=True)

        owner_row = owner_in[...].astype(F32)
        owner_col = column_of(owner_row)
        tiles = cells_in[...]
        cell_row = ((tiles & 1) * cols + (tiles >> 1)).astype(F32)
        cell_col = column_of(cell_row)
        alike = jnp.where(owner_col == owner_row, 1.0, 0.0)
        rank_col = jnp.sum(jnp.where(lane < sub, alike, 0.0), axis=1, keepdims=True)
        rank_row = jnp.sum(jnp.where(sub < lane, alike, 0.0), axis=0, keepdims=True)

        def flags(condition):
            return jnp.where(condition, 1.0, 0.0).astype(BF16)

        named = owner_row == sub.astype(F32)
        slot_zero = flags(named & (rank_row == 0.0))
        slot_one = flags(named & (rank_row == 1.0))
        taking = owner_col == lane.astype(F32)
        slot_zero_t = flags(taking & (rank_col == 0.0))
        slot_one_t = flags(taking & (rank_col == 1.0))
        at_cell = flags(cell_col == iota((count, 2 * cols), 1).astype(F32))
        at_cell_t = flags(cell_row == iota((2 * cols, count), 0).astype(F32))
        pick[0:count, :] = product(slot_zero, at_cell).astype(BF16)
        pick[count : 2 * count, :] = product(slot_one, at_cell).astype(BF16)
        unpick[:, 0:count] = product(at_cell_t, slot_zero_t).astype(BF16)
        unpick[:, count : 2 * count] = product(at_cell_t, slot_one_t).astype(BF16)

        offsets = offsets_in[...].astype(F32).astype(BF16)

        def offsets_of(slot):
            return lax.dot_general(
                slot, offsets, (((1,), (1,)), ((), ())), preferred_element_type=F32
            )

        off = jnp.concatenate([offsets_of(slot_zero), offsets_of(slot_one)], axis=1)
        off = off.astype(jnp.int32)
        off_ref[...] = off

        half = TILE // 2
        place = lane & (half - 1)
        base = lane & half
        key = off * half + place
        length = 2
        while length <= half:
            d = length // 2
            while d >= 1:
                partner = lanes_at(key, lane ^ d)
                lower = jnp.where((lane & d) == 0, 1, 0)
                upward = jnp.where((place & length) == 0, 1, 0)
                key = jnp.where(
                    lower == upward, jnp.minimum(key, partner), jnp.maximum(key, partner)
                )
                d //= 2
            length *= 2
        perm_ref[...] = base | (key & (half - 1))
        ordered = key >> 6
        d = 1
        level = 0
        while d < half:
            together = (place >= d) & (shift_lanes(ordered, d) == ordered)
            same_ref[level] = jnp.where(together, 1.0, 0.0).astype(F32)
            d *= 2
            level += 1
        for k in range(2):
            found = jnp.zeros((count, TILE), jnp.int32)
            jump = half // 2
            while jump >= 1:
                seen = lanes_at(ordered, found + (k * half + jump - 1))
                found = jnp.where(seen <= lane, found + jump, found)
                jump //= 2
            seen = lanes_at(ordered, found + k * half)
            found = jnp.where(seen <= lane, found + 1, found)
            last = jnp.maximum(found - 1, 0) + k * half
            hit = (found > 0) & (lanes_at(ordered, last) == lane)
            last_ref[k] = last
            some_ref[k] = jnp.where(hit, 1.0, 0.0).astype(F32)

    row_at = iota((plane, nz), 0)
    z_at = iota((plane, nz), 1)

    def next_y(values, row):
        return jnp.where(row_at == plane - 1, row, shift_rows(values, -1))

    def prior_y(values, row):
        return jnp.where(row_at == 0, row, shift_rows(values, 1))

    def next_z(values):
        return jnp.where(z_at == nz - 1, 0.0, shift_lanes(values, -1))

    def prior_z(values):
        return jnp.where(z_at == 0, 0.0, shift_lanes(values, 1))

    def step_h():
        keep_x = jnp.where(mx == gx - 1, 0.0, 1.0).astype(F32)
        keep_y = jnp.where(my == gy - 1, 0.0, 1.0).astype(F32)
        for c in (1, 2):
            ep[c, cols : cols + plane, :] = ep[c, cols : cols + plane, :] * keep_x
        for x in range(cx):
            here = slice(x * plane, (x + 1) * plane)
            after = slice((x + 1) * plane, (x + 2) * plane)
            e0, e1, e2 = ep[0, here, :], ep[1, here, :], ep[2, here, :]
            e1_x, e2_x = ep[1, after, :], ep[2, after, :]
            e0_y = next_y(e0, halo_e[0, x : x + 1, :] * keep_y)
            e2_y = next_y(e2, halo_e[1, x : x + 1, :] * keep_y)
            hp[0, after, :] = hp[0, after, :] - COURANT * ((e2_y - e2) - (next_z(e1) - e1))
            hp[1, after, :] = hp[1, after, :] - COURANT * ((next_z(e0) - e0) - (e2_x - e2))
            hp[2, after, :] = hp[2, after, :] - COURANT * ((e1_x - e1) - (e0_y - e0))
            bottom = slice((x + 2) * plane - 1, (x + 2) * plane)
            row_h[0, x : x + 1, :] = hp[0, bottom, :]
            row_h[1, x : x + 1, :] = hp[2, bottom, :]

    def step_e():
        hold_x = jnp.where(mx == 0, 0.0, 1.0).astype(F32)
        hold_y = jnp.where(my == 0, 0.0, 1.0).astype(F32)
        for c in (1, 2):
            hp[c, 0:plane, :] = hp[c, 0:plane, :] * hold_x
        for x in range(cx):
            here = slice(x * plane, (x + 1) * plane)
            after = slice((x + 1) * plane, (x + 2) * plane)
            h0, h1, h2 = hp[0, after, :], hp[1, after, :], hp[2, after, :]
            h1_x, h2_x = hp[1, here, :], hp[2, here, :]
            h0_y = prior_y(h0, halo_h[0, x : x + 1, :] * hold_y)
            h2_y = prior_y(h2, halo_h[1, x : x + 1, :] * hold_y)
            ep[0, here, :] = ep[0, here, :] + COURANT * ((h2 - h2_y) - (h1 - prior_z(h1)))
            ep[1, here, :] = ep[1, here, :] + COURANT * ((h0 - prior_z(h0)) - (h2 - h2_x))
            ep[2, here, :] = ep[2, here, :] + COURANT * ((h1 - h1_x) - (h0 - h0_y))

    def dipole_rows(c):
        return dip_recv[pl.ds(c, count, stride=4), :]

    def sampled_drive():
        drive = jnp.zeros((count, TILE), F32)
        for c in range(3):
            rows = jnp.zeros((2 * count, 2 * TILE), F32)
            for h in range(2):
                parts = jnp.concatenate(split(ep[c, 0:cols, h * TILE : (h + 1) * TILE]), axis=1)
                rows = rows + product(pick[:, h * cols : (h + 1) * cols], parts)
            rows = rows[:, 0:TILE] + rows[:, TILE : 2 * TILE]
            sample = jnp.where(
                lane < TILE // 2,
                lanes_at(rows[0:count], off_ref[...]),
                lanes_at(rows[count : 2 * count], off_ref[...]),
            )
            drive = drive + dipole_rows(c) * sample
        return drive * TIME_STEP

    def feed_field(moved):
        for c in range(3):
            sums = lanes_at(moved * dipole_rows(c), perm_ref[...])
            d = 1
            level = 0
            while d < TILE // 2:
                sums = sums + same_ref[level] * shift_lanes(sums, d)
                d *= 2
                level += 1
            rows = [lanes_at(sums, last_ref[k]) * some_ref[k] for k in range(2)]
            parts = jnp.concatenate(split(jnp.concatenate(rows, axis=0)), axis=1)
            change = product(unpick[...], parts)
            change = change[:, 0:TILE] + change[:, TILE : 2 * TILE]
            for h in range(2):
                part = slice(h * TILE, (h + 1) * TILE)
                ep[c, 0:cols, part] = ep[c, 0:cols, part] - change[h * cols : (h + 1) * cols, :]

    def advance(step, start, number):
        height = pairs + 32 if step == 0 else pairs

        def look(g):
            part = pl.ds(pl.multiple_of((start + WIDTH * g) * TILE, WIDTH * TILE), WIDTH * TILE)
            return product(
                later_ref[0:height, :], stacked(dens[0:pairs, part], dens[pairs : 2 * pairs, part])
            )

        rounds = number // WIDTH

        def one(g, out):
            after = look(jnp.minimum(g + 1, rounds - 1))
            keep = keep_ref[...]
            spacing = spacing_ref[...]
            for w in range(WIDTH):
                s = start + WIDTH * g + w
                part = pl.ds(pl.multiple_of(s * TILE, TILE), TILE)
                left = slice(w * TILE, (w + 1) * TILE)
                right = slice((WIDTH + w) * TILE, (WIDTH + w + 1) * TILE)
                real = dens[0:pairs, part]
                imag = dens[pairs : 2 * pairs, part]
                force = drive_recv[pl.ds(step * count + s, 1), :]
                dens[0:pairs, part] = keep * real + spacing * imag + force * out[0:pairs, right]
                dens[pairs : 2 * pairs, part] = (
                    keep * imag - spacing * real - force * out[0:pairs, left]
                )
                if step == 0:
                    seen = out[pairs : pairs + 16, left] + out[pairs + 16 : pairs + 32, right]
                    rows = pl.ds(pl.multiple_of(s * 8, 8), 8)
                    ahead[rows, :] = seen[0:8, :] + force * seen[8:16, :]
            return after

        lax.fori_loop(0, rounds, one, look(0), unroll=UNROLL)

    def drive_of(step):
        return drive_send[step * count : (step + 1) * count, :]

    def moved_at(step):
        recv, width = coefs[step][1], coefs[step][2]
        terms = [recv[pl.ds(k, count, stride=width), :] for k in range(width)]
        back = step - (width.bit_length() - 2)
        while len(terms) > 1:
            half = len(terms) // 2
            force = drive_of(back)
            terms = [terms[k] + force * terms[k + half] for k in range(half)]
            back += 1
        return terms[0]

    def until_h(step):
        e_plane.wait_recv()
        e_row.wait_recv()
        step_h()
        h_row.start()
        h_plane.start()

    def until_drive(step):
        e_plane.wait_send()
        e_row.wait_send()
        h_plane.wait_recv()
        h_row.wait_recv()
        step_e()
        if step == 0:
            all_dip.wait_recv()
        drive_send[step * count : (step + 1) * count, :] = sampled_drive()
        h_plane.wait_send()
        h_row.wait_send()

    def until_e(step):
        all_coef(step).wait_recv()
        feed_field(moved_at(step))
        if step < STEPS - 1:
            send_e()

    half = count // 2
    quarter = count // 4

    find_places()
    until_h(0)
    look_first()
    send_coef(0)
    until_drive(0)
    until_e(0)
    send_drive(0)
    send_coef(1)
    until_h(1)
    all_drive(0).wait_recv()
    combine(coef2_send, looked, 8, 16, 0)
    send_coef(2)
    until_drive(1)
    until_e(1)
    send_drive(1)
    advance(0, 0, half)
    until_h(2)
    advance(0, half, half)
    all_drive(1).wait_recv()
    combine(coef3_send, ahead, 0, 8, 1)
    send_coef(3)
    until_drive(2)
    until_e(2)
    send_drive(2)
    advance(1, 0, half)
    until_h(3)
    advance(1, half, half)
    all_drive(2).wait_recv()
    advance(2, 0, quarter)
    until_drive(3)
    send_drive(3)
    until_e(3)
    advance(2, quarter, count - quarter)
    all_drive(3).wait_recv()
    all_dip.wait_send()
    for step in range(STEPS):
        all_drive(step).wait_send()
        all_coef(step).wait_send()


def finish(
    gx,
    gy,
    plane,
    ep,
    hp,
    dens,
    drive_recv,
    later_ref,
    keep_ref,
    spacing_ref,
    e_out,
    h_out,
    dens_out,
    fresh,
    out_sem,
    field_sem,
):
    count = gx * gy
    cols = e_out.shape[1]
    pairs = dens.shape[0] // 2
    group = gy * TILE
    wide = WIDTH * TILE
    field_stores = (
        pltpu.make_async_copy(ep.at[:, 0:cols, :], e_out, field_sem.at[0]),
        pltpu.make_async_copy(hp.at[:, plane : plane + cols, :], h_out, field_sem.at[1]),
    )
    for copy in field_stores:
        copy.start()

    def store_group(g):
        part = pl.ds(pl.multiple_of(g * group, group), group)
        return pltpu.make_async_copy(fresh.at[:, part], dens_out.at[:, part], out_sem.at[g])

    def look(g):
        part = pl.ds(pl.multiple_of(g * wide, wide), wide)
        return product(
            later_ref[0:pairs, :], stacked(dens[0:pairs, part], dens[pairs : 2 * pairs, part])
        )

    rounds = count // WIDTH
    per_group = gy // WIDTH

    def one_group(group_at, out):
        for i in range(per_group):
            g = group_at * per_group + i
            after = look(jnp.minimum(g + 1, rounds - 1))
            keep = keep_ref[...]
            spacing = spacing_ref[...]
            for w in range(WIDTH):
                s = WIDTH * g + w
                part = pl.ds(pl.multiple_of(s * TILE, TILE), TILE)
                left = slice(w * TILE, (w + 1) * TILE)
                right = slice((WIDTH + w) * TILE, (WIDTH + w + 1) * TILE)
                real = dens[0:pairs, part]
                imag = dens[pairs : 2 * pairs, part]
                force = drive_recv[pl.ds((STEPS - 1) * count + s, 1), :]
                fresh[0:pairs, part] = keep * real + spacing * imag + force * out[:, right]
                fresh[pairs : 2 * pairs, part] = (
                    keep * imag - spacing * real - force * out[:, left]
                )
            out = after
        store_group(group_at).start()
        return out

    lax.fori_loop(0, gx, one_group, look(0))
    for copy in field_stores:
        copy.wait()

    @pl.loop(0, gx)
    def _(g):
        store_group(g).wait()


def body(
    field_e,
    field_h,
    density,
    dipole,
    levels,
    coupling,
    rates,
    tile_cells,
    tile_owner,
    emitter_offsets,
):
    gx = lax.axis_size("gx")
    gy = lax.axis_size("gy")
    count = gx * gy
    _, cx, cy, nz = field_e.shape
    cols = cx * cy
    pairs = coupling.shape[0] ** 2
    columns = density.shape[3]

    size = coupling.shape[0]
    vmem = pl.BlockSpec(memory_space=pltpu.VMEM)
    hbm = pl.BlockSpec(memory_space=pltpu.HBM)
    dma = pltpu.SemaphoreType.DMA
    tall = (count, TILE)
    padded = jax.ShapeDtypeStruct((3, cols + cy, nz), F32)
    state = pl.pallas_call(
        functools.partial(kernel, gx, gy, cx, cy),
        out_shape=(
            padded,
            padded,
            jax.ShapeDtypeStruct((2 * pairs, columns), F32),
            jax.ShapeDtypeStruct((STEPS * count, TILE), F32),
            jax.ShapeDtypeStruct((pairs + 32, 3 * pairs), BF16),
            jax.ShapeDtypeStruct((pairs, TILE), F32),
            jax.ShapeDtypeStruct((pairs, TILE), F32),
        ),
        in_specs=[hbm] * 10,
        out_specs=(vmem,) * 7,
        scratch_shapes=[
            pltpu.VMEM((1, size), F32),
            pltpu.VMEM((size, size), F32),
            pltpu.VMEM((size, size), F32),
            pltpu.VMEM((1, count), jnp.int32),
            pltpu.VMEM((1, count), jnp.int32),
            pltpu.VMEM((TILE // 2, count), jnp.int32),
            pltpu.VMEM((3, columns), F32),
            pltpu.VMEM((2 * count, 2 * cols), BF16),
            pltpu.VMEM((2 * cols, 2 * count), BF16),
            pltpu.VMEM(tall, jnp.int32),
            pltpu.VMEM(tall, jnp.int32),
            pltpu.VMEM((2,) + tall, jnp.int32),
            pltpu.VMEM((2,) + tall, F32),
            pltpu.VMEM((6,) + tall, F32),
            pltpu.VMEM((32, 3 * pairs), BF16),
            pltpu.VMEM((2, cx, nz), F32),
            pltpu.VMEM((2, cx, nz), F32),
            pltpu.VMEM((2, cx, nz), F32),
            pltpu.VMEM((2, cx, nz), F32),
            pltpu.VMEM((4 * count, TILE), F32),
            pltpu.VMEM((4 * count, TILE), F32),
            pltpu.VMEM((STEPS * count, TILE), F32),
            pltpu.VMEM((2 * count, TILE), F32),
            pltpu.VMEM((2 * count, TILE), F32),
            pltpu.VMEM((4 * count, TILE), F32),
            pltpu.VMEM((4 * count, TILE), F32),
            pltpu.VMEM((4 * count, TILE), F32),
            pltpu.VMEM((4 * count, TILE), F32),
            pltpu.VMEM((4 * count, TILE), F32),
            pltpu.VMEM((4 * count, TILE), F32),
            pltpu.VMEM((16 * count, TILE), F32),
            pltpu.VMEM((8 * count, TILE), F32),
            dma((4,)),
            dma((4,)),
            dma((2,)),
            dma((STEPS,)),
            dma((STEPS,)),
            dma((STEPS,)),
            dma((STEPS,)),
            dma((gx,)),
            dma((6,)),
            dma((3,)),
        ],
        compiler_params=pltpu.CompilerParams(
            collective_id=0, has_side_effects=True, vmem_limit_bytes=24 * 1024 * 1024
        ),
    )(*(pltpu.with_memory_space_constraint(x, pltpu.HBM) for x in (
        levels.reshape(1, -1),
        coupling,
        rates,
        tile_cells.reshape(1, -1),
        tile_owner.reshape(1, -1),
        emitter_offsets.T,
        field_e.reshape(3, cols, nz),
        field_h.reshape(3, cols, nz),
        density.reshape(2 * pairs, columns),
        dipole,
    )))
    e_out, h_out, dens_out = pl.pallas_call(
        functools.partial(finish, gx, gy, cy),
        out_shape=(
            jax.ShapeDtypeStruct((3, cols, nz), F32),
            jax.ShapeDtypeStruct((3, cols, nz), F32),
            jax.ShapeDtypeStruct((2 * pairs, columns), F32),
        ),
        in_specs=[vmem] * 7,
        out_specs=(hbm, hbm, hbm),
        scratch_shapes=[
            pltpu.VMEM((2 * pairs, columns), F32),
            dma((gx,)),
            dma((2,)),
        ],
        compiler_params=pltpu.CompilerParams(vmem_limit_bytes=24 * 1024 * 1024),
    )(*state)
    return (
        e_out.reshape(field_e.shape),
        h_out.reshape(field_h.shape),
        dens_out.reshape(density.shape),
    )


def solution(mesh):
    placed = (
        P(None, "gx", "gy", None),
        P(None, "gx", "gy", None),
        P(None, None, None, ("gx", "gy")),
        P(None, ("gx", "gy")),
        P(),
        P(),
        P(),
        P(("gx", "gy")),
        P(("gx", "gy"), None),
        P(("gx", "gy"), None),
    )
    return jax.shard_map(
        body,
        mesh=mesh,
        in_specs=placed,
        out_specs=(
            P(None, "gx", "gy", None),
            P(None, "gx", "gy", None),
            P(None, None, None, ("gx", "gy")),
        ),
        check_vma=False,
    )
```

```python
import functools

import jax
import jax.numpy as jnp
from jax import lax
from jax.experimental import pallas as pl
from jax.experimental.pallas import tpu as pltpu
from jax.sharding import PartitionSpec as P

TILE = 128
STEPS = 4
COURANT = 0.5
TIME_STEP = 0.12
WIDTH = 2
FIRST = 4
UNROLL = 4

MESH = pl.DeviceIdType.MESH
F32 = jnp.float32
BF16 = jnp.bfloat16


def iota(shape, axis):
    return lax.broadcasted_iota(jnp.int32, shape, axis)


def lanes_at(values, index):
    return jnp.take_along_axis(values, index, axis=1, mode="promise_in_bounds")


def split(values):
    high = values.astype(BF16)
    return high, (values - high.astype(F32)).astype(BF16)


def product(left, right):
    return jnp.dot(left, right, preferred_element_type=F32)


def stacked(real, imag):
    real_high, real_low = split(real)
    imag_high, imag_low = split(imag)
    high = jnp.concatenate([real_high, imag_high], axis=1)
    low = jnp.concatenate([real_low, imag_low], axis=1)
    return jnp.concatenate([high, low, high], axis=0)


def exact(left, right):
    return jnp.dot(left, right, preferred_element_type=F32, precision=lax.Precision.HIGHEST)


def exact_t(left, right):
    return lax.dot_general(
        left,
        right,
        (((1,), (1,)), ((), ())),
        preferred_element_type=F32,
        precision=lax.Precision.HIGHEST,
    )


def shift_rows(values, amount):
    return pltpu.roll(values, amount % values.shape[0], 0)


def shift_lanes(values, amount):
    return pltpu.roll(values, amount % values.shape[1], 1)


def level_constants(levels, coupling, rates, size):
    pairs = size * size
    first = jnp.where(iota((pairs, size), 0) // size == iota((pairs, size), 1), 1.0, 0.0).astype(F32)
    second = jnp.where(iota((pairs, size), 0) % size == iota((pairs, size), 1), 1.0, 0.0).astype(F32)
    row_at, col_at = iota((pairs, pairs), 0), iota((pairs, pairs), 1)
    eye = jnp.where(row_at == col_at, 1.0, 0.0).astype(F32)

    def pair_of(pick):
        half = exact(pick, coupling)
        return 0.5 * (exact_t(half, pick) + exact_t(pick, half))

    def symmetrized(values):
        return 0.5 * (
            jnp.sum(exact(first, values) * second, axis=1, keepdims=True)
            + jnp.sum(exact(second, values) * first, axis=1, keepdims=True)
        )

    def as_row(column):
        return jnp.sum(eye * column, axis=0, keepdims=True)

    commute = jnp.where(row_at % size == col_at % size, pair_of(first), 0.0) - jnp.where(
        row_at // size == col_at // size, pair_of(second), 0.0
    )
    sym = symmetrized(coupling)
    off_diagonal = jnp.where(
        iota((pairs, 1), 0) // size == iota((pairs, 1), 0) % size, 0.0, 1.0
    ).astype(F32)
    decay = TIME_STEP * symmetrized(rates) * off_diagonal
    spacing = TIME_STEP * jnp.sum((first - second) * levels, axis=1, keepdims=True)

    sym_row, decay_row, spacing_row = as_row(sym), as_row(decay), as_row(spacing)
    rows = iota((16, pairs), 0)

    def free(real, imag):
        keep = 1.0 - decay_row
        return real * keep - imag * spacing_row, real * spacing_row + imag * keep

    def driven(real, imag):
        return -exact(imag, commute), exact(real, commute)

    def both(real, imag, distance):
        free_real, free_imag = free(real, imag)
        driven_real, driven_imag = driven(real, imag)
        return (
            free_real + shift_rows(driven_real, distance),
            free_imag + shift_rows(driven_imag, distance),
        )

    push = exact(jnp.broadcast_to(sym_row, (16, pairs)), commute)
    real_zero = jnp.where(rows == 0, -sym_row * decay_row, 0.0)
    imag_zero = jnp.where(rows == 0, sym_row * spacing_row, jnp.where(rows == 1, push, 0.0))
    real_one, imag_one = both(real_zero, imag_zero, 2)
    real_two, imag_two = both(real_one, imag_one, 4)
    real_three, imag_three = both(real_two, imag_two, 8)

    def parts(matrix):
        high, low = split(matrix)
        return jnp.concatenate([high, high, low], axis=1)

    def opening(zero, one, two):
        return one + shift_rows(zero, 4) + shift_rows(two, 8)

    begin = parts(
        jnp.concatenate(
            [opening(real_zero, real_one, real_two), opening(imag_zero, imag_one, imag_two)],
            axis=0,
        )
    )
    later = parts(jnp.concatenate([commute, real_three, imag_three], axis=0))
    keep = jnp.broadcast_to(1.0 - decay, (pairs, TILE))
    spacing = jnp.broadcast_to(spacing, (pairs, TILE))
    return begin, later, keep, spacing


def kernel(
    gx,
    gy,
    cx,
    cy,
    levels_hbm,
    coupling_hbm,
    rates_hbm,
    cells_hbm,
    owner_hbm,
    offsets_hbm,
    e_in,
    h_in,
    dens_in,
    dip_in,
    ep,
    hp,
    dens,
    drive_recv,
    later_ref,
    keep_ref,
    spacing_ref,
    levels_in,
    coupling_in,
    rates_in,
    cells_in,
    owner_in,
    offsets_in,
    dip_mine,
    pick,
    unpick,
    off_ref,
    perm_ref,
    last_ref,
    some_ref,
    same_ref,
    begin_ref,
    row_e,
    row_h,
    halo_e,
    halo_h,
    dip_send,
    dip_recv,
    drive_send,
    coef0_send,
    coef0_recv,
    coef1_send,
    coef1_recv,
    coef2_send,
    coef2_recv,
    coef3_send,
    coef3_recv,
    looked,
    ahead,
    halo_send,
    halo_recv,
    dip_sems,
    drive_ssem,
    drive_rsem,
    coef_ssem,
    coef_rsem,
    in_sem,
    small_sem,
    field_sem,
):
    mx = lax.axis_index("gx")
    my = lax.axis_index("gy")
    me = mx * gy + my
    count = gx * gy
    plane = cy
    cols = cx * cy
    nz = 2 * TILE
    group = gy * TILE
    size = levels_in.shape[1]
    pairs = size * size

    def load_group(g):
        part = pl.ds(pl.multiple_of(g * group, group), group)
        return pltpu.make_async_copy(dens_in.at[:, part], dens.at[:, part], in_sem.at[g])

    field_loads = (
        pltpu.make_async_copy(e_in, ep.at[:, 0:cols, :], field_sem.at[0]),
        pltpu.make_async_copy(h_in, hp.at[:, plane : plane + cols, :], field_sem.at[1]),
    )
    small_loads = [
        pltpu.make_async_copy(source, target, small_sem.at[i])
        for i, (source, target) in enumerate(
            (
                (levels_hbm, levels_in),
                (coupling_hbm, coupling_in),
                (rates_hbm, rates_in),
                (cells_hbm, cells_in),
                (owner_hbm, owner_in),
                (offsets_hbm, offsets_in),
            )
        )
    ]
    dip_load = pltpu.make_async_copy(dip_in, dip_mine, field_sem.at[2])

    def along_x(j):
        return lax.rem(mx + j, gx)

    def along_y(j):
        return lax.rem(my + j, gy)

    def device_of(number):
        return number >> (gy.bit_length() - 1), number & (gy - 1)

    def other(j):
        return (me + j) & (count - 1)

    def to_all(source, target, base, step_of, width, send_sem, recv_sem):
        def one(j, carry):
            peer = other(j)
            pltpu.make_async_remote_copy(
                src_ref=source.at[pl.ds(base + peer * step_of, width), :],
                dst_ref=target.at[pl.ds(base + me * step_of, width), :],
                send_sem=send_sem,
                recv_sem=recv_sem,
                device_id=device_of(peer),
                device_id_type=MESH,
            ).start()
            return carry

        lax.fori_loop(1, count, one, 0, unroll=8)
        own = pl.ds(base + me * step_of, width)
        target[own, :] = source[own, :]

    def whole(source, target, base, width, send_sem, recv_sem):
        rows = pl.ds(base, (count - 1) * width)
        return pltpu.make_async_remote_copy(
            src_ref=source.at[rows, :],
            dst_ref=target.at[rows, :],
            send_sem=send_sem,
            recv_sem=recv_sem,
            device_id=(along_x(1), my),
            device_id_type=MESH,
        )

    drive_sems = [(drive_ssem.at[step], drive_rsem.at[step]) for step in range(STEPS)]
    coefs = [
        (send, recv, width, coef_ssem.at[step], coef_rsem.at[step])
        for step, (send, recv, width) in enumerate(
            (
                (coef0_send, coef0_recv, 2),
                (coef1_send, coef1_recv, 4),
                (coef2_send, coef2_recv, 4),
                (coef3_send, coef3_recv, 4),
            )
        )
    ]

    def all_drive(step):
        return whole(drive_send, drive_recv, step * count, 1, *drive_sems[step])

    def send_drive(step):
        to_all(drive_send, drive_recv, step * count, 1, 1, *drive_sems[step])

    def all_coef(step):
        send, recv, width, out_sem, back_sem = coefs[step]
        return whole(send, recv, 0, width, out_sem, back_sem)

    def send_coef(step):
        send, recv, width, out_sem, back_sem = coefs[step]
        to_all(send, recv, 0, width, width, out_sem, back_sem)

    all_dip = whole(dip_send, dip_recv, 0, 4, dip_sems.at[0], dip_sems.at[1])

    x_below, x_above = along_x(gx - 1), along_x(1)
    y_below, y_above = along_y(gy - 1), along_y(1)

    def halo_copy(which, source, target, device):
        return pltpu.make_async_remote_copy(
            src_ref=source,
            dst_ref=target,
            send_sem=halo_send.at[which],
            recv_sem=halo_recv.at[which],
            device_id=device,
            device_id_type=MESH,
        )

    e_plane = halo_copy(
        0, ep.at[1:3, 0:plane, :], ep.at[1:3, cols : cols + plane, :], (x_below, my)
    )
    e_row = halo_copy(1, row_e, halo_e, (mx, y_below))
    h_plane = halo_copy(
        2, hp.at[1:3, cols : cols + plane, :], hp.at[1:3, 0:plane, :], (x_above, my)
    )
    h_row = halo_copy(3, row_h, halo_h, (mx, y_above))

    def send_e():
        for x in range(cx):
            row_e[0, x : x + 1, :] = ep[0, x * plane : x * plane + 1, :]
            row_e[1, x : x + 1, :] = ep[2, x * plane : x * plane + 1, :]
        e_row.start()
        e_plane.start()

    for copy in small_loads:
        copy.start()
    dip_load.start()
    for copy in field_loads:
        copy.start()

    @pl.loop(0, gx)
    def _(g):
        load_group(g).start()

    barrier = pltpu.get_barrier_semaphore()

    def greet(j, carry):
        pl.semaphore_signal(barrier, inc=1, device_id=device_of(other(j)), device_id_type=MESH)
        return carry

    lax.fori_loop(1, count, greet, 0, unroll=8)

    for copy in small_loads:
        copy.wait()
    begin, later, keep, spacing = level_constants(
        levels_in[...], coupling_in[...], rates_in[...], size
    )
    begin_ref[...] = begin
    later_ref[...] = later
    keep_ref[...] = keep
    spacing_ref[...] = spacing

    dip_load.wait()

    def dip_row(s, carry):
        lanes = pl.ds(pl.multiple_of(s * TILE, TILE), TILE)
        dip_send[pl.ds(pl.multiple_of(s * 4, 4), 3), :] = dip_mine[:, lanes]
        return carry

    dip_send[pl.ds(3, count, stride=4), :] = jnp.zeros((count, TILE), F32)
    lax.fori_loop(0, count, dip_row, 0, unroll=8)
    for copy in field_loads:
        copy.wait()


    def look_first():
        @pl.loop(0, gx)
        def _(g):
            load_group(g).wait()

        def one(g, carry):
            part = pl.ds(pl.multiple_of(g * FIRST * TILE, FIRST * TILE), FIRST * TILE)
            state = stacked(dens[0:pairs, part], dens[pairs : 2 * pairs, part])
            seen = product(begin_ref[...], state)
            seen = seen[0:16, 0 : FIRST * TILE] + seen[16:32, FIRST * TILE :]
            for w in range(FIRST):
                rows = pl.ds(pl.multiple_of((g * FIRST + w) * 16, 16), 16)
                looked[rows, :] = seen[:, w * TILE : (w + 1) * TILE]
            return carry

        lax.fori_loop(0, count // FIRST, one, 0, unroll=4)
        for k in range(4):
            coef1_send[pl.ds(k, count, stride=4), :] = looked[pl.ds(k, count, stride=16), :]
        for k in range(2):
            coef0_send[pl.ds(k, count, stride=2), :] = looked[pl.ds(4 + k, count, stride=16), :]

    def combine(target, source, first, stride, step):
        force = drive_recv[step * count : (step + 1) * count, :]
        for k in range(4):
            target[pl.ds(k, count, stride=4), :] = (
                source[pl.ds(first + k, count, stride=stride), :]
                + force * source[pl.ds(first + k + 4, count, stride=stride), :]
            )

    lane = iota((count, TILE), 1)
    sub = iota((count, TILE), 0)

    def find_places():
        eye = jnp.where(lane == sub, 1.0, 0.0).astype(F32)

        def column_of(row):
            return jnp.sum(eye * row, axis=1, keepdims=True)

        owner_row = owner_in[...].astype(F32)
        owner_col = column_of(owner_row)
        tiles = cells_in[...]
        cell_row = ((tiles & 1) * cols + (tiles >> 1)).astype(F32)
        cell_col = column_of(cell_row)
        alike = jnp.where(owner_col == owner_row, 1.0, 0.0)
        rank_col = jnp.sum(jnp.where(lane < sub, alike, 0.0), axis=1, keepdims=True)
        rank_row = jnp.sum(jnp.where(sub < lane, alike, 0.0), axis=0, keepdims=True)

        def flags(condition):
            return jnp.where(condition, 1.0, 0.0).astype(BF16)

        named = owner_row == sub.astype(F32)
        slot_zero = flags(named & (rank_row == 0.0))
        slot_one = flags(named & (rank_row == 1.0))
        taking = owner_col == lane.astype(F32)
        slot_zero_t = flags(taking & (rank_col == 0.0))
        slot_one_t = flags(taking & (rank_col == 1.0))
        at_cell = flags(cell_col == iota((count, 2 * cols), 1).astype(F32))
        at_cell_t = flags(cell_row == iota((2 * cols, count), 0).astype(F32))
        pick[0:count, :] = product(slot_zero, at_cell).astype(BF16)
        pick[count : 2 * count, :] = product(slot_one, at_cell).astype(BF16)
        unpick[:, 0:count] = product(at_cell_t, slot_zero_t).astype(BF16)
        unpick[:, count : 2 * count] = product(at_cell_t, slot_one_t).astype(BF16)

        offsets = offsets_in[...].astype(F32).astype(BF16)

        def offsets_of(slot):
            return lax.dot_general(
                slot, offsets, (((1,), (1,)), ((), ())), preferred_element_type=F32
            )

        off = jnp.concatenate([offsets_of(slot_zero), offsets_of(slot_one)], axis=1)
        off = off.astype(jnp.int32)
        off_ref[...] = off

        half = TILE // 2
        place = lane & (half - 1)
        base = lane & half
        key = off * half + place
        length = 2
        while length <= half:
            d = length // 2
            while d >= 1:
                partner = lanes_at(key, lane ^ d)
                lower = jnp.where((lane & d) == 0, 1, 0)
                upward = jnp.where((place & length) == 0, 1, 0)
                key = jnp.where(
                    lower == upward, jnp.minimum(key, partner), jnp.maximum(key, partner)
                )
                d //= 2
            length *= 2
        perm_ref[...] = base | (key & (half - 1))
        ordered = key >> 6
        d = 1
        level = 0
        while d < half:
            together = (place >= d) & (shift_lanes(ordered, d) == ordered)
            same_ref[level] = jnp.where(together, 1.0, 0.0).astype(F32)
            d *= 2
            level += 1
        for k in range(2):
            found = jnp.zeros((count, TILE), jnp.int32)
            jump = half // 2
            while jump >= 1:
                seen = lanes_at(ordered, found + (k * half + jump - 1))
                found = jnp.where(seen <= lane, found + jump, found)
                jump //= 2
            seen = lanes_at(ordered, found + k * half)
            found = jnp.where(seen <= lane, found + 1, found)
            last = jnp.maximum(found - 1, 0) + k * half
            hit = (found > 0) & (lanes_at(ordered, last) == lane)
            last_ref[k] = last
            some_ref[k] = jnp.where(hit, 1.0, 0.0).astype(F32)

    row_at = iota((plane, nz), 0)
    z_at = iota((plane, nz), 1)

    def next_y(values, row):
        return jnp.where(row_at == plane - 1, row, shift_rows(values, -1))

    def prior_y(values, row):
        return jnp.where(row_at == 0, row, shift_rows(values, 1))

    def next_z(values):
        return jnp.where(z_at == nz - 1, 0.0, shift_lanes(values, -1))

    def prior_z(values):
        return jnp.where(z_at == 0, 0.0, shift_lanes(values, 1))

    def step_h():
        keep_x = jnp.where(mx == gx - 1, 0.0, 1.0).astype(F32)
        keep_y = jnp.where(my == gy - 1, 0.0, 1.0).astype(F32)
        for c in (1, 2):
            ep[c, cols : cols + plane, :] = ep[c, cols : cols + plane, :] * keep_x
        for x in range(cx):
            here = slice(x * plane, (x + 1) * plane)
            after = slice((x + 1) * plane, (x + 2) * plane)
            e0, e1, e2 = ep[0, here, :], ep[1, here, :], ep[2, here, :]
            e1_x, e2_x = ep[1, after, :], ep[2, after, :]
            e0_y = next_y(e0, halo_e[0, x : x + 1, :] * keep_y)
            e2_y = next_y(e2, halo_e[1, x : x + 1, :] * keep_y)
            hp[0, after, :] = hp[0, after, :] - COURANT * ((e2_y - e2) - (next_z(e1) - e1))
            hp[1, after, :] = hp[1, after, :] - COURANT * ((next_z(e0) - e0) - (e2_x - e2))
            hp[2, after, :] = hp[2, after, :] - COURANT * ((e1_x - e1) - (e0_y - e0))
            bottom = slice((x + 2) * plane - 1, (x + 2) * plane)
            row_h[0, x : x + 1, :] = hp[0, bottom, :]
            row_h[1, x : x + 1, :] = hp[2, bottom, :]

    def step_e():
        hold_x = jnp.where(mx == 0, 0.0, 1.0).astype(F32)
        hold_y = jnp.where(my == 0, 0.0, 1.0).astype(F32)
        for c in (1, 2):
            hp[c, 0:plane, :] = hp[c, 0:plane, :] * hold_x
        for x in range(cx):
            here = slice(x * plane, (x + 1) * plane)
            after = slice((x + 1) * plane, (x + 2) * plane)
            h0, h1, h2 = hp[0, after, :], hp[1, after, :], hp[2, after, :]
            h1_x, h2_x = hp[1, here, :], hp[2, here, :]
            h0_y = prior_y(h0, halo_h[0, x : x + 1, :] * hold_y)
            h2_y = prior_y(h2, halo_h[1, x : x + 1, :] * hold_y)
            ep[0, here, :] = ep[0, here, :] + COURANT * ((h2 - h2_y) - (h1 - prior_z(h1)))
            ep[1, here, :] = ep[1, here, :] + COURANT * ((h0 - prior_z(h0)) - (h2 - h2_x))
            ep[2, here, :] = ep[2, here, :] + COURANT * ((h1 - h1_x) - (h0 - h0_y))

    def dipole_rows(c):
        return dip_recv[pl.ds(c, count, stride=4), :]

    def sampled_drive():
        drive = jnp.zeros((count, TILE), F32)
        for c in range(3):
            rows = jnp.zeros((2 * count, 2 * TILE), F32)
            for h in range(2):
                parts = jnp.concatenate(split(ep[c, 0:cols, h * TILE : (h + 1) * TILE]), axis=1)
                rows = rows + product(pick[:, h * cols : (h + 1) * cols], parts)
            rows = rows[:, 0:TILE] + rows[:, TILE : 2 * TILE]
            sample = jnp.where(
                lane < TILE // 2,
                lanes_at(rows[0:count], off_ref[...]),
                lanes_at(rows[count : 2 * count], off_ref[...]),
            )
            drive = drive + dipole_rows(c) * sample
        return drive * TIME_STEP

    def feed_field(moved):
        for c in range(3):
            sums = lanes_at(moved * dipole_rows(c), perm_ref[...])
            d = 1
            level = 0
            while d < TILE // 2:
                sums = sums + same_ref[level] * shift_lanes(sums, d)
                d *= 2
                level += 1
            rows = [lanes_at(sums, last_ref[k]) * some_ref[k] for k in range(2)]
            parts = jnp.concatenate(split(jnp.concatenate(rows, axis=0)), axis=1)
            change = product(unpick[...], parts)
            change = change[:, 0:TILE] + change[:, TILE : 2 * TILE]
            for h in range(2):
                part = slice(h * TILE, (h + 1) * TILE)
                ep[c, 0:cols, part] = ep[c, 0:cols, part] - change[h * cols : (h + 1) * cols, :]

    def advance(step, start, number):
        height = pairs + 32 if step == 0 else pairs

        def look(g):
            part = pl.ds(pl.multiple_of((start + WIDTH * g) * TILE, WIDTH * TILE), WIDTH * TILE)
            return product(
                later_ref[0:height, :], stacked(dens[0:pairs, part], dens[pairs : 2 * pairs, part])
            )

        rounds = number // WIDTH

        def one(g, out):
            after = look(jnp.minimum(g + 1, rounds - 1))
            keep = keep_ref[...]
            spacing = spacing_ref[...]
            for w in range(WIDTH):
                s = start + WIDTH * g + w
                part = pl.ds(pl.multiple_of(s * TILE, TILE), TILE)
                left = slice(w * TILE, (w + 1) * TILE)
                right = slice((WIDTH + w) * TILE, (WIDTH + w + 1) * TILE)
                real = dens[0:pairs, part]
                imag = dens[pairs : 2 * pairs, part]
                force = drive_recv[pl.ds(step * count + s, 1), :]
                dens[0:pairs, part] = keep * real + spacing * imag + force * out[0:pairs, right]
                dens[pairs : 2 * pairs, part] = (
                    keep * imag - spacing * real - force * out[0:pairs, left]
                )
                if step == 0:
                    seen = out[pairs : pairs + 16, left] + out[pairs + 16 : pairs + 32, right]
                    rows = pl.ds(pl.multiple_of(s * 8, 8), 8)
                    ahead[rows, :] = seen[0:8, :] + force * seen[8:16, :]
            return after

        lax.fori_loop(0, rounds, one, look(0), unroll=UNROLL)

    def drive_of(step):
        return drive_send[step * count : (step + 1) * count, :]

    def moved_at(step):
        recv, width = coefs[step][1], coefs[step][2]
        terms = [recv[pl.ds(k, count, stride=width), :] for k in range(width)]
        back = step - (width.bit_length() - 2)
        while len(terms) > 1:
            half = len(terms) // 2
            force = drive_of(back)
            terms = [terms[k] + force * terms[k + half] for k in range(half)]
            back += 1
        return terms[0]

    def until_h(step):
        e_plane.wait_recv()
        e_row.wait_recv()
        step_h()
        h_row.start()
        h_plane.start()

    def until_drive(step):
        e_plane.wait_send()
        e_row.wait_send()
        h_plane.wait_recv()
        h_row.wait_recv()
        step_e()
        if step == 0:
            all_dip.wait_recv()
        drive_send[step * count : (step + 1) * count, :] = sampled_drive()
        h_plane.wait_send()
        h_row.wait_send()

    def until_e(step):
        all_coef(step).wait_recv()
        feed_field(moved_at(step))
        if step < STEPS - 1:
            send_e()

    find_places()
    pl.semaphore_wait(barrier, count - 1)
    send_e()
    to_all(dip_send, dip_recv, 0, 4, 4, dip_sems.at[0], dip_sems.at[1])

    half = count // 2
    quarter = count // 4

    look_first()
    until_h(0)
    send_coef(0)
    until_drive(0)
    until_e(0)
    send_drive(0)
    send_coef(1)
    until_h(1)
    all_drive(0).wait_recv()
    combine(coef2_send, looked, 8, 16, 0)
    send_coef(2)
    until_drive(1)
    until_e(1)
    send_drive(1)
    advance(0, 0, half)
    until_h(2)
    advance(0, half, half)
    all_drive(1).wait_recv()
    combine(coef3_send, ahead, 0, 8, 1)
    send_coef(3)
    until_drive(2)
    until_e(2)
    send_drive(2)
    advance(1, 0, half)
    until_h(3)
    advance(1, half, half)
    all_drive(2).wait_recv()
    advance(2, 0, quarter)
    until_drive(3)
    send_drive(3)
    until_e(3)
    advance(2, quarter, count - quarter)
    all_drive(3).wait_recv()
    all_dip.wait_send()
    for step in range(STEPS):
        all_drive(step).wait_send()
        all_coef(step).wait_send()


def finish(
    gx,
    gy,
    plane,
    ep,
    hp,
    dens,
    drive_recv,
    later_ref,
    keep_ref,
    spacing_ref,
    e_out,
    h_out,
    dens_out,
    fresh,
    out_sem,
    field_sem,
):
    count = gx * gy
    cols = e_out.shape[1]
    pairs = dens.shape[0] // 2
    group = gy * TILE
    wide = WIDTH * TILE
    field_stores = (
        pltpu.make_async_copy(ep.at[:, 0:cols, :], e_out, field_sem.at[0]),
        pltpu.make_async_copy(hp.at[:, plane : plane + cols, :], h_out, field_sem.at[1]),
    )
    for copy in field_stores:
        copy.start()

    def store_group(g):
        part = pl.ds(pl.multiple_of(g * group, group), group)
        return pltpu.make_async_copy(fresh.at[:, part], dens_out.at[:, part], out_sem.at[g])

    def look(g):
        part = pl.ds(pl.multiple_of(g * wide, wide), wide)
        return product(
            later_ref[0:pairs, :], stacked(dens[0:pairs, part], dens[pairs : 2 * pairs, part])
        )

    rounds = count // WIDTH
    per_group = gy // WIDTH

    def one_group(group_at, out):
        for i in range(per_group):
            g = group_at * per_group + i
            after = look(jnp.minimum(g + 1, rounds - 1))
            keep = keep_ref[...]
            spacing = spacing_ref[...]
            for w in range(WIDTH):
                s = WIDTH * g + w
                part = pl.ds(pl.multiple_of(s * TILE, TILE), TILE)
                left = slice(w * TILE, (w + 1) * TILE)
                right = slice((WIDTH + w) * TILE, (WIDTH + w + 1) * TILE)
                real = dens[0:pairs, part]
                imag = dens[pairs : 2 * pairs, part]
                force = drive_recv[pl.ds((STEPS - 1) * count + s, 1), :]
                fresh[0:pairs, part] = keep * real + spacing * imag + force * out[:, right]
                fresh[pairs : 2 * pairs, part] = (
                    keep * imag - spacing * real - force * out[:, left]
                )
            out = after
        store_group(group_at).start()
        return out

    lax.fori_loop(0, gx, one_group, look(0))
    for copy in field_stores:
        copy.wait()

    @pl.loop(0, gx)
    def _(g):
        store_group(g).wait()


def body(
    field_e,
    field_h,
    density,
    dipole,
    levels,
    coupling,
    rates,
    tile_cells,
    tile_owner,
    emitter_offsets,
):
    gx = lax.axis_size("gx")
    gy = lax.axis_size("gy")
    count = gx * gy
    _, cx, cy, nz = field_e.shape
    cols = cx * cy
    pairs = coupling.shape[0] ** 2
    columns = density.shape[3]

    size = coupling.shape[0]
    vmem = pl.BlockSpec(memory_space=pltpu.VMEM)
    hbm = pl.BlockSpec(memory_space=pltpu.HBM)
    dma = pltpu.SemaphoreType.DMA
    tall = (count, TILE)
    padded = jax.ShapeDtypeStruct((3, cols + cy, nz), F32)
    state = pl.pallas_call(
        functools.partial(kernel, gx, gy, cx, cy),
        out_shape=(
            padded,
            padded,
            jax.ShapeDtypeStruct((2 * pairs, columns), F32),
            jax.ShapeDtypeStruct((STEPS * count, TILE), F32),
            jax.ShapeDtypeStruct((pairs + 32, 3 * pairs), BF16),
            jax.ShapeDtypeStruct((pairs, TILE), F32),
            jax.ShapeDtypeStruct((pairs, TILE), F32),
        ),
        in_specs=[hbm] * 10,
        out_specs=(vmem,) * 7,
        scratch_shapes=[
            pltpu.VMEM((1, size), F32),
            pltpu.VMEM((size, size), F32),
            pltpu.VMEM((size, size), F32),
            pltpu.VMEM((1, count), jnp.int32),
            pltpu.VMEM((1, count), jnp.int32),
            pltpu.VMEM((TILE // 2, count), jnp.int32),
            pltpu.VMEM((3, columns), F32),
            pltpu.VMEM((2 * count, 2 * cols), BF16),
            pltpu.VMEM((2 * cols, 2 * count), BF16),
            pltpu.VMEM(tall, jnp.int32),
            pltpu.VMEM(tall, jnp.int32),
            pltpu.VMEM((2,) + tall, jnp.int32),
            pltpu.VMEM((2,) + tall, F32),
            pltpu.VMEM((6,) + tall, F32),
            pltpu.VMEM((32, 3 * pairs), BF16),
            pltpu.VMEM((2, cx, nz), F32),
            pltpu.VMEM((2, cx, nz), F32),
            pltpu.VMEM((2, cx, nz), F32),
            pltpu.VMEM((2, cx, nz), F32),
            pltpu.VMEM((4 * count, TILE), F32),
            pltpu.VMEM((4 * count, TILE), F32),
            pltpu.VMEM((STEPS * count, TILE), F32),
            pltpu.VMEM((2 * count, TILE), F32),
            pltpu.VMEM((2 * count, TILE), F32),
            pltpu.VMEM((4 * count, TILE), F32),
            pltpu.VMEM((4 * count, TILE), F32),
            pltpu.VMEM((4 * count, TILE), F32),
            pltpu.VMEM((4 * count, TILE), F32),
            pltpu.VMEM((4 * count, TILE), F32),
            pltpu.VMEM((4 * count, TILE), F32),
            pltpu.VMEM((16 * count, TILE), F32),
            pltpu.VMEM((8 * count, TILE), F32),
            dma((4,)),
            dma((4,)),
            dma((2,)),
            dma((STEPS,)),
            dma((STEPS,)),
            dma((STEPS,)),
            dma((STEPS,)),
            dma((gx,)),
            dma((6,)),
            dma((3,)),
        ],
        compiler_params=pltpu.CompilerParams(
            collective_id=0, has_side_effects=True, vmem_limit_bytes=24 * 1024 * 1024
        ),
    )(*(pltpu.with_memory_space_constraint(x, pltpu.HBM) for x in (
        levels.reshape(1, -1),
        coupling,
        rates,
        tile_cells.reshape(1, -1),
        tile_owner.reshape(1, -1),
        emitter_offsets.T,
        field_e.reshape(3, cols, nz),
        field_h.reshape(3, cols, nz),
        density.reshape(2 * pairs, columns),
        dipole,
    )))
    e_out, h_out, dens_out = pl.pallas_call(
        functools.partial(finish, gx, gy, cy),
        out_shape=(
            jax.ShapeDtypeStruct((3, cols, nz), F32),
            jax.ShapeDtypeStruct((3, cols, nz), F32),
            jax.ShapeDtypeStruct((2 * pairs, columns), F32),
        ),
        in_specs=[vmem] * 7,
        out_specs=(hbm, hbm, hbm),
        scratch_shapes=[
            pltpu.VMEM((2 * pairs, columns), F32),
            dma((gx,)),
            dma((2,)),
        ],
        compiler_params=pltpu.CompilerParams(vmem_limit_bytes=24 * 1024 * 1024),
    )(*state)
    return (
        e_out.reshape(field_e.shape),
        h_out.reshape(field_h.shape),
        dens_out.reshape(density.shape),
    )


def solution(mesh):
    placed = (
        P(None, "gx", "gy", None),
        P(None, "gx", "gy", None),
        P(None, None, None, ("gx", "gy")),
        P(None, ("gx", "gy")),
        P(),
        P(),
        P(),
        P(("gx", "gy")),
        P(("gx", "gy"), None),
        P(("gx", "gy"), None),
    )
    return jax.shard_map(
        body,
        mesh=mesh,
        in_specs=placed,
        out_specs=(
            P(None, "gx", "gy", None),
            P(None, "gx", "gy", None),
            P(None, None, None, ("gx", "gy")),
        ),
        check_vma=False,
    )
```
